128 devices in a mesh: ctx: 16 (over y, x_hi, core), tp: 8 (over x_lo, z).
Axes of the slice: x: 4 (x_hi: 2, x_lo: 2; x = x_hi * 2 + x_lo), y: 4, z: 4, core: 2. Of those that a mesh axis runs over, the one named last changes fastest.
Arguments:
- hyena_query: bfloat16 [6144, 8192], P('ctx', 'tp'), may hold values from -6 to 6
- hyena_key: bfloat16 [6144, 8192], P('ctx', 'tp'), may hold values from -6 to 6
- hyena_value: bfloat16 [6144, 8192], P('ctx', 'tp'), may hold values from -6 to 6
- conv_filter: bfloat16 [512, 128], P('tp'), may hold values from -0.5 to 0.5
- skip_gain: float32 [8192], P('tp'), may hold values from -4 to 4
- query_rows: bfloat16 [6144, 8192], P('ctx', 'tp'), may hold values from -80 to 80
- key_rows: bfloat16 [6144, 8192], P('ctx', 'tp'), may hold values from -4 to 4, as said below
- value_rows: bfloat16 [6144, 8192], P('ctx', 'tp'), may hold values from -6 to 6
- out_weight: bfloat16 [8192, 8192], P(None, 'tp'), may hold values from -1 to 1
Outputs:
- hyena_out: bfloat16 [6144, 8192], P('ctx', 'tp')
- attention_out: bfloat16 [8192, 6144], P('tp', 'ctx')
The draws below stay inside these ranges and needn't reach their ends.
Inputs may be any that keep to these rules, and one draw needn't show every extreme that they name: `key_rows`: keys of order one.
All inputs are finite; a program needn't handle non-finite values.
Results may differ from the reference program's by a relative error of at most 0.014.
Values may be sent and summed in bfloat16 or wider, within the bound.
No kernel may reach another device: no remote copies, remote signals or barrier semaphores. Data moves between devices by JAX's collectives and lax.ppermute only.
A program may use at most 128 MiB of HBM per device.

```python
import jax
import jax.numpy as jnp
import numpy as np
from jax import lax

D = 8192
HEADS = 64
HEAD_DIM = 128
FILTER_LEN = 128
SEQ_LEN = 6144
GROUPS = 512
N_TP = 8


def paired_rows(key):
    base = jax.random.fold_in(key, 11)
    first_key, second_key = jax.random.split(base, 2)
    keys_drawn = jnp.clip(jax.random.normal(first_key, (SEQ_LEN, D), jnp.float32), -4.0, 4.0)
    queries_drawn = jnp.clip(jax.random.normal(second_key, (SEQ_LEN, D), jnp.float32), -4.0, 4.0)
    return (queries_drawn, keys_drawn)


def draw_query_rows(key, part):
    return paired_rows(key)[0].astype(jnp.bfloat16)


def draw_key_rows(key, part):
    return paired_rows(key)[1].astype(jnp.bfloat16)


def with_spikes(array, own_key, source, target, blocks, factor):
    owner, partner = [(jnp.arange(array.shape[dim]) // (array.shape[dim] // blocks)).reshape([-1 if axis == dim else 1 for axis in range(array.ndim)]) for dim in (source, target)]
    chosen = jax.random.permutation(own_key, blocks)[partner]
    strong = (owner == chosen) | (owner == (partner + blocks // 2) % blocks)
    return jnp.where(strong, factor * array, array)


def block_scale(key, shape, cuts, low, top_value):
    level = 1.0
    for axis_at, parts in cuts:
        heights = jax.random.uniform(jax.random.fold_in(jax.random.fold_in(key, 6), axis_at), (parts,), jnp.float32, low / len(cuts), top_value / len(cuts))
        level = level * jnp.repeat(jnp.exp(heights), shape[axis_at] // parts).reshape((-1,) + (1,) * (len(shape) - 1 - axis_at))
    return level


def scatter_about(stream_key, extent, spread, limit, cuts=(), kind=jnp.bfloat16):
    values = spread * jax.random.normal(stream_key, extent, jnp.float32)
    if cuts:
        values = values * block_scale(stream_key, extent, cuts, -0.22, 0.18)
    return jnp.clip(values, -limit, limit).astype(kind)


def noise_with(rng, dims, deviation, bound, cuts, heavy, held_as=jnp.bfloat16):
    values = deviation * jax.random.normal(rng, dims, jnp.float32)
    if cuts:
        values = values * block_scale(rng, dims, cuts, -0.22, 0.18)
    return jnp.clip(with_spikes(values, jax.random.fold_in(rng, 3), *heavy), -bound, bound).astype(held_as)


def setup_inputs(seed: int = 0) -> dict:
    arg_keys = jax.random.split(jax.random.key(seed), 10)
    return {
        "hyena_query": scatter_about(arg_keys[0], (SEQ_LEN, D), 1.0, 6.0, ((0, 16), (1, 8))),
        "hyena_key": scatter_about(arg_keys[1], (SEQ_LEN, D), 1.0, 6.0, ((0, 16), (1, 8))),
        "hyena_value": scatter_about(arg_keys[2], (SEQ_LEN, D), 1.0, 6.0, ((0, 16), (1, 8))),
        "conv_filter": scatter_about(arg_keys[3], (GROUPS, FILTER_LEN), FILTER_LEN ** -0.5, 0.5, ((0, 8),)),
        "skip_gain": scatter_about(arg_keys[4], (D,), 1.0, 4.0, ((0, 8),), jnp.float32),
        "query_rows": draw_query_rows(jax.random.fold_in(arg_keys[9], 71), 0),
        "key_rows": draw_key_rows(jax.random.fold_in(arg_keys[9], 71), 0),
        "value_rows": scatter_about(arg_keys[7], (SEQ_LEN, D), 1.0, 6.0, ((0, 16), (1, 8))),
        "out_weight": noise_with(arg_keys[8], (D, D), HEADS ** -0.5, 1.0, ((1, 8),), (1, 0, 8, 2.0)),
    }


top_precision = lax.Precision.HIGHEST


def toeplitz_pair(filters):
    length = filters.shape[1]
    lag_table = np.arange(length)[:, None] - np.arange(length)[None, :]
    inner_index = np.clip(lag_table, 0, length - 1)
    outer_index = np.clip(lag_table + length, 0, length - 1)
    inner_part = jnp.where(jnp.asarray(lag_table >= 0)[None], filters[:, inner_index], jnp.zeros((), filters.dtype))
    outer_part = jnp.where(jnp.asarray(lag_table < 0)[None], filters[:, outer_index], jnp.zeros((), filters.dtype))
    return inner_part, outer_part


def grouped_conv(current, before, filters):
    blocks, length, feature_width = current.shape
    groups = filters.shape[0]
    inner_part, outer_part = toeplitz_pair(filters)
    inner_part = inner_part.astype(jnp.float32)
    outer_part = outer_part.astype(jnp.float32)
    split_shape = (blocks, length, groups, feature_width // groups)
    result = jnp.einsum("gts,bsgc->btgc", inner_part, current.reshape(split_shape), precision=top_precision)
    result = result + jnp.einsum("gts,bsgc->btgc", outer_part, before.reshape(split_shape), precision=top_precision)
    return result.reshape(blocks * length, feature_width)


def reference(hyena_query, hyena_key, hyena_value, conv_filter, skip_gain, query_rows, key_rows, value_rows, out_weight):
    product = (hyena_key.astype(jnp.float32) * hyena_value.astype(jnp.float32)).astype(jnp.bfloat16)
    widened = lax.optimization_barrier(product).astype(jnp.float32)
    blocks = SEQ_LEN // FILTER_LEN
    current = widened.reshape(blocks, FILTER_LEN, D)
    before = jnp.concatenate([jnp.zeros_like(current[:1]), current[:-1]], axis=0)
    convolved = grouped_conv(current, before, conv_filter)
    hyena_out = (hyena_query.astype(jnp.float32) * (convolved + skip_gain[None, :] * widened)).astype(jnp.bfloat16)

    score_scale = HEAD_DIM ** -0.5
    positions = jnp.arange(SEQ_LEN, dtype=jnp.int32)
    allowed = positions[None, :] <= positions[:, None]

    def one_head(head_index):
        first_col = head_index * HEAD_DIM
        query_part = lax.dynamic_slice_in_dim(query_rows, first_col, HEAD_DIM, 1).astype(jnp.float32)
        key_part = lax.dynamic_slice_in_dim(key_rows, first_col, HEAD_DIM, 1).astype(jnp.float32)
        value_part = lax.dynamic_slice_in_dim(value_rows, first_col, HEAD_DIM, 1).astype(jnp.float32)
        scores = jnp.dot(query_part, key_part.T, precision=top_precision) * score_scale
        scores = jnp.where(allowed, scores, -jnp.inf)
        row_top = jnp.max(scores, axis=1, keepdims=True)
        weights = jnp.exp(scores - row_top)
        row_total = jnp.sum(weights, axis=1, keepdims=True)
        probs = lax.optimization_barrier(weights.astype(jnp.bfloat16)).astype(jnp.float32)
        mixed_rows = jnp.dot(probs, value_part, precision=top_precision)
        return (mixed_rows / row_total).astype(jnp.bfloat16)

    per_head = lax.map(one_head, jnp.arange(HEADS, dtype=jnp.int32))
    attended = jnp.transpose(per_head, (1, 0, 2)).reshape(SEQ_LEN, D)

    group_share = D // N_TP
    attention_out = jnp.zeros((D, SEQ_LEN), jnp.float32)
    for group_index in range(N_TP):
        weight_part = out_weight[:, group_index * group_share:(group_index + 1) * group_share].astype(jnp.float32)
        rows_part = attended[:, group_index * group_share:(group_index + 1) * group_share].astype(jnp.float32)
        partial_sum = jnp.dot(weight_part, rows_part.T, precision=top_precision)
        rounded = lax.optimization_barrier(partial_sum.astype(jnp.bfloat16))
        attention_out = attention_out + rounded.astype(jnp.float32)
    return hyena_out, attention_out.astype(jnp.bfloat16)
```

```python
import jax
import jax.numpy as jnp
from jax import lax
from jax.experimental import pallas as pl
from jax.experimental.pallas import tpu as pltpu
from jax.sharding import PartitionSpec as P

HEAD_DIM = 128
CHIPS_Y = 4
CHIPS = 8
RING = 4
NEGATIVE = -1e30
EXP_SCALE = HEAD_DIM ** (-0.5) * 1.4426950408889634


VMEM = pltpu.VMEM
SMEM_SPEC = pl.BlockSpec(memory_space=pltpu.SMEM)
VMEM_SPEC = pl.BlockSpec(memory_space=pltpu.VMEM)


def shifted(block, axis, distance):
    devices = range(lax.axis_size(axis))
    route = [(i - distance, i) for i in devices if i - distance in devices]
    return lax.ppermute(block, axis, route)


def toeplitz_pair(filters):
    length = filters.shape[1]
    lag_table = (
        jnp.arange(length, dtype=jnp.int32)[:, None] - jnp.arange(length, dtype=jnp.int32)[None, :]
    )
    taps = jnp.arange(length, dtype=jnp.int32)[:, None, None]
    inner_table = (lag_table[None] == taps).astype(jnp.bfloat16)
    outer_table = (lag_table[None] + length == taps).astype(jnp.bfloat16)
    inner_part = jnp.einsum(
        "gj,jts->gts", filters, inner_table, preferred_element_type=jnp.float32
    ).astype(jnp.bfloat16)
    outer_part = jnp.einsum(
        "gj,jts->gts", filters, outer_table, preferred_element_type=jnp.float32
    ).astype(jnp.bfloat16)
    return (inner_part, outer_part)


def local_conv(current, before, filters):
    blocks, length, feature_width = current.shape
    groups = filters.shape[0]
    split_shape = (blocks, length, groups, feature_width // groups)
    inner_part, outer_part = toeplitz_pair(filters)
    result = jnp.einsum(
        "gts,bsgc->btgc",
        inner_part,
        current.reshape(split_shape),
        preferred_element_type=jnp.float32,
    )
    result = result + jnp.einsum(
        "gts,bsgc->btgc",
        outer_part,
        before.reshape(split_shape),
        preferred_element_type=jnp.float32,
    )
    return result.reshape(blocks * length, feature_width)


def hyena(hyena_query, hyena_key, hyena_value, conv_filter, skip_gain):
    product = (hyena_key.astype(jnp.float32) * hyena_value.astype(jnp.float32)).astype(jnp.bfloat16)
    length = conv_filter.shape[1]
    tokens_here, feature_width = product.shape
    blocks = tokens_here // length
    previous = shifted(product[tokens_here - length :], "ctx", 1)
    widened = product.astype(jnp.float32)
    earlier = jnp.concatenate([previous, product[: tokens_here - length]], axis=0)
    convolved = local_conv(
        product.reshape(blocks, length, feature_width),
        earlier.reshape(blocks, length, feature_width),
        conv_filter,
    )
    return (hyena_query.astype(jnp.float32) * (convolved + skip_gain[None, :] * widened)).astype(
        jnp.bfloat16
    )


def chip_route(step):
    route = []
    for source in range(2 * CHIPS):
        y, x, core = source // 4, source // 2 % 2, source % 2
        target = ((y + step // 2) % CHIPS_Y * 2 + (x + step) % 2) * 2 + core
        route.append((source, target))
    return route


CORE_ROUTE = [(i, i ^ 1) for i in range(2 * CHIPS)]


def ring_route(step):
    return [(i, i // RING * RING + (i + step) % RING) for i in range(2 * RING)]


PAIR_ROUTE = [(i, (i + RING) % (2 * RING)) for i in range(2 * RING)]


def ahead(y, x, step):
    return ((y + step // 2) & 3) * 2 + ((x + step) & 1)


def behind(y, x, step):
    return ((y - step // 2) & 3) * 2 + ((x - step) & 1)


def split_kernel(place, q_ref, k_ref, v_ref, *outs):
    y, x = place[0], place[1]
    rows = q_ref.shape[0]
    for step in range(CHIPS):
        column = pl.multiple_of(ahead(y, x, step) * HEAD_DIM, HEAD_DIM)
        outs[step][:rows, :] = k_ref[:, pl.ds(column, HEAD_DIM)]
        outs[step][rows:, :] = v_ref[:, pl.ds(column, HEAD_DIM)]
        outs[CHIPS + step][...] = q_ref[:, pl.ds(column, HEAD_DIM)]


def split_heads(place, query_rows, key_rows, value_rows):
    rows = query_rows.shape[0]
    outs = [jax.ShapeDtypeStruct((2 * rows, HEAD_DIM), jnp.bfloat16)] * CHIPS
    outs += [jax.ShapeDtypeStruct((rows, HEAD_DIM), jnp.bfloat16)] * CHIPS
    return pl.pallas_call(
        split_kernel,
        out_shape=outs,
        in_specs=[SMEM_SPEC] + [VMEM_SPEC] * 3,
        out_specs=[VMEM_SPEC] * (2 * CHIPS),
        name="split_heads",
    )(place, query_rows, key_rows, value_rows)


def attention_kernel(place, *refs):
    queries = refs[:CHIPS]
    own = refs[CHIPS : 2 * CHIPS]
    other = refs[2 * CHIPS : 3 * CHIPS]
    outs = refs[3 * CHIPS : 4 * CHIPS]
    q_now, keys, values, top, total = refs[4 * CHIPS :]
    y, x, core = place[0], place[1], place[2]
    step = pl.program_id(0)
    rows = q_now.shape[0]

    @pl.when(step == 0)
    def _():
        ones = jnp.ones((2 * rows, HEAD_DIM), jnp.bfloat16)
        for i in range(CHIPS):
            keys[i, :rows, :] = own[i][:rows, :]
            keys[i, rows:, :] = other[i][:rows, :]
            values[i, :rows, :HEAD_DIM] = own[i][rows:, :]
            values[i, rows:, :HEAD_DIM] = other[i][rows:, :]
            values[i, :, HEAD_DIM:] = ones

    for i in range(CHIPS):

        @pl.when(step == i)
        def _(i=i):
            q_now[...] = queries[(8 - i if i % 2 == 0 else 10 - i) % 8 if i else 0][...]

    top[...] = jnp.full_like(top, NEGATIVE)
    total[...] = jnp.zeros_like(total)
    chip = ahead(y, x, step)

    def update(block_keys, block_values, masked):
        width = block_keys.shape[0]
        scores = lax.dot_general(
            q_now[...],
            block_keys,
            (((1,), (1,)), ((), ())),
            preferred_element_type=jnp.float32,
        )
        if masked:
            row = lax.broadcasted_iota(jnp.int32, scores.shape, 0)
            column = lax.broadcasted_iota(jnp.int32, scores.shape, 1)
            scores = jnp.where(column <= row, scores, NEGATIVE)
        old = top[...]
        new = jnp.maximum(old, jnp.max(scores, axis=1, keepdims=True))
        keep = jnp.exp2((old - new) * EXP_SCALE)
        spread = jnp.concatenate([new] * (width // HEAD_DIM), axis=1)
        weights = jnp.exp2((scores - spread) * EXP_SCALE).astype(jnp.bfloat16)
        total[...] = total[...] * jnp.concatenate([keep, keep], axis=1) + jnp.dot(
            weights, block_values, preferred_element_type=jnp.float32
        )
        top[...] = new

    def slot_of(other_chip):
        return ((y - (other_chip >> 1)) & 3) * 2 + ((x - other_chip) & 1)

    def full_step(j, unused):
        slot = slot_of(j)
        update(keys[slot], values[slot], False)
        return unused

    lax.fori_loop(0, chip, full_step, 0)
    last = slot_of(chip)
    update(keys[last, :rows, :], values[last, :rows, :], True)

    @pl.when(core == 1)
    def _():
        update(keys[last, rows:, :], values[last, rows:, :], False)

    result = (total[:, :HEAD_DIM] / total[:, HEAD_DIM:]).astype(jnp.bfloat16)
    for i in range(CHIPS):

        @pl.when(step == i)
        def _(i=i):
            outs[i][...] = result


def attention(place, queries, own, other):
    rows = queries[0].shape[0]
    return pl.pallas_call(
        attention_kernel,
        grid=(CHIPS,),
        out_shape=[jax.ShapeDtypeStruct((rows, HEAD_DIM), jnp.bfloat16)] * CHIPS,
        in_specs=[SMEM_SPEC] + [VMEM_SPEC] * (3 * CHIPS),
        out_specs=[VMEM_SPEC] * CHIPS,
        scratch_shapes=[
            VMEM((rows, HEAD_DIM), jnp.bfloat16),
            VMEM((CHIPS, 2 * rows, HEAD_DIM), jnp.bfloat16),
            VMEM((CHIPS, 2 * rows, 2 * HEAD_DIM), jnp.bfloat16),
            VMEM((rows, HEAD_DIM), jnp.float32),
            VMEM((rows, 2 * HEAD_DIM), jnp.float32),
        ],
        cost_estimate=pl.CostEstimate(
            flops=12_000_000_000, bytes_accessed=6_000_000, transcendentals=10_000_000
        ),
        name="attention",
    )(place, *queries, *own, *other)


def join_kernel(place, *refs):
    y, x = place[0], place[1]
    joined = refs[CHIPS]
    for step in range(CHIPS):
        column = pl.multiple_of(behind(y, x, step) * HEAD_DIM, HEAD_DIM)
        joined[:, pl.ds(column, HEAD_DIM)] = refs[step][...]


def join_heads(place, pieces):
    rows = pieces[0].shape[0]
    return pl.pallas_call(
        join_kernel,
        out_shape=jax.ShapeDtypeStruct((rows, CHIPS * HEAD_DIM), jnp.bfloat16),
        in_specs=[SMEM_SPEC] + [VMEM_SPEC] * CHIPS,
        out_specs=VMEM_SPEC,
        name="join_heads",
    )(place, *pieces)


def project(place, wanted, out_weight, attended):
    rows, features = attended.shape
    share = out_weight.shape[0] // (4 * RING)

    def weight_block(step, place):
        index = jnp.int32(0)
        for i, (x_off, z_off, half) in enumerate(wanted):
            row = ((((place[3] + x_off) & 1) * RING + ((place[4] + z_off) & 3)) * 2) + half
            index = jnp.where(step == i, row, index)
        return (index, 0)

    def kernel(place, weight_ref, attended_ref, *outs):
        piece = lax.dot_general(
            weight_ref[...],
            attended_ref[...],
            (((1,), (1,)), ((), ())),
            preferred_element_type=jnp.float32,
        ).astype(jnp.bfloat16)
        for i in range(len(wanted)):

            @pl.when(pl.program_id(0) == i)
            def _(i=i):
                outs[i][...] = piece

    count = len(wanted)
    return pl.pallas_call(
        kernel,
        grid_spec=pltpu.PrefetchScalarGridSpec(
            num_scalar_prefetch=1,
            grid=(count,),
            in_specs=[
                pl.BlockSpec((share, features), weight_block),
                pl.BlockSpec((rows, features), lambda step, place: (0, 0)),
            ],
            out_specs=[pl.BlockSpec((share, rows), lambda step, place: (0, 0))] * count,
        ),
        out_shape=[jax.ShapeDtypeStruct((share, rows), jnp.bfloat16)] * count,
        cost_estimate=pl.CostEstimate(
            flops=2 * share * rows * features * count,
            bytes_accessed=share * features * 2 * count,
            transcendentals=0,
        ),
        name="project",
    )(place, out_weight, attended)


def added(*pieces):
    return sum(piece.astype(jnp.float32) for piece in pieces)


def local(
    hyena_query,
    hyena_key,
    hyena_value,
    conv_filter,
    skip_gain,
    query_rows,
    key_rows,
    value_rows,
    out_weight,
):
    ctx = lax.axis_index("ctx")
    tp = lax.axis_index("tp")
    place = jnp.stack([ctx // 4, ctx // 2 % 2, ctx % 2, tp // RING, tp % RING]).astype(jnp.int32)

    pieces = split_heads(place, query_rows, key_rows, value_rows)
    own = [pieces[0]] + [
        lax.ppermute(pieces[step], "ctx", chip_route(step)) for step in range(1, CHIPS)
    ]
    queries = [pieces[CHIPS]] + [
        lax.ppermute(pieces[CHIPS + step], "ctx", chip_route(step)) for step in range(1, CHIPS)
    ]
    other = [lax.ppermute(block, "ctx", CORE_ROUTE) for block in own]
    hyena_out = hyena(hyena_query, hyena_key, hyena_value, conv_filter, skip_gain)
    outs = attention(place, queries, own, other)
    back = [outs[0]] + [
        lax.ppermute(outs[step], "ctx", chip_route(step)) for step in range(1, CHIPS)
    ]
    attended = join_heads(place, back)

    kept = []
    handed = None
    for x_off in (1, 0):
        far = project(place, [(x_off, 2, 0), (x_off, 2, 1)], out_weight, attended)
        near = project(
            place,
            [
                (x_off, 1, 1),
                (x_off, 3, 0),
                (x_off, 1, 0),
                (x_off, 3, 1),
                (x_off, 0, 0),
                (x_off, 0, 1),
            ],
            out_weight,
            attended,
        )
        from_below = lax.ppermute(far[0], "tp", ring_route(1))
        from_above = lax.ppermute(far[1], "tp", ring_route(-1))
        below_1 = lax.ppermute(near[0], "tp", ring_route(1))
        above_0 = lax.ppermute(near[1], "tp", ring_route(-1))
        up = added(near[2], from_below).astype(jnp.bfloat16)
        down = added(near[3], from_above).astype(jnp.bfloat16)
        below_0 = lax.ppermute(up, "tp", ring_route(1))
        above_1 = lax.ppermute(down, "tp", ring_route(-1))
        first = added(near[4], below_0, above_0)
        second = added(near[5], below_1, above_1)
        if x_off == 1:
            handed = [
                lax.ppermute(part.astype(jnp.bfloat16), "tp", PAIR_ROUTE)
                for part in (first, second)
            ]
        else:
            kept = [first, second]
    attention_out = jnp.concatenate(
        [(kept[i] + handed[i].astype(jnp.float32)).astype(jnp.bfloat16) for i in range(2)], axis=0
    )
    return (hyena_out, attention_out)


def solution(mesh):
    in_specs = (
        P("ctx", "tp"),
        P("ctx", "tp"),
        P("ctx", "tp"),
        P("tp", None),
        P("tp"),
        P("ctx", "tp"),
        P("ctx", "tp"),
        P("ctx", "tp"),
        P(None, "tp"),
    )
    out_specs = (P("ctx", "tp"), P("tp", "ctx"))
    return jax.shard_map(local, mesh=mesh, in_specs=in_specs, out_specs=out_specs, check_vma=False)
```

```python
import jax
import jax.numpy as jnp
from jax import lax
from jax.experimental import pallas as pl
from jax.experimental.pallas import tpu as pltpu
from jax.sharding import PartitionSpec as P

HEAD_DIM = 128
CHIPS_Y = 4
CHIPS = 8
RING = 4
NEGATIVE = -1e30
EXP_SCALE = HEAD_DIM ** (-0.5) * 1.4426950408889634


VMEM = pltpu.VMEM
SMEM_SPEC = pl.BlockSpec(memory_space=pltpu.SMEM)
VMEM_SPEC = pl.BlockSpec(memory_space=pltpu.VMEM)


def shifted(block, axis, distance):
    devices = range(lax.axis_size(axis))
    route = [(i - distance, i) for i in devices if i - distance in devices]
    return lax.ppermute(block, axis, route)


def toeplitz_pair(filters):
    length = filters.shape[1]
    lag_table = (
        jnp.arange(length, dtype=jnp.int32)[:, None] - jnp.arange(length, dtype=jnp.int32)[None, :]
    )
    taps = jnp.arange(length, dtype=jnp.int32)[:, None, None]
    inner_table = (lag_table[None] == taps).astype(jnp.bfloat16)
    outer_table = (lag_table[None] + length == taps).astype(jnp.bfloat16)
    inner_part = jnp.einsum(
        "gj,jts->gts", filters, inner_table, preferred_element_type=jnp.float32
    ).astype(jnp.bfloat16)
    outer_part = jnp.einsum(
        "gj,jts->gts", filters, outer_table, preferred_element_type=jnp.float32
    ).astype(jnp.bfloat16)
    return (inner_part, outer_part)


def local_conv(current, before, filters):
    blocks, length, feature_width = current.shape
    groups = filters.shape[0]
    split_shape = (blocks, length, groups, feature_width // groups)
    inner_part, outer_part = toeplitz_pair(filters)
    result = jnp.einsum(
        "gts,bsgc->btgc",
        inner_part,
        current.reshape(split_shape),
        preferred_element_type=jnp.float32,
    )
    result = result + jnp.einsum(
        "gts,bsgc->btgc",
        outer_part,
        before.reshape(split_shape),
        preferred_element_type=jnp.float32,
    )
    return result.reshape(blocks * length, feature_width)


def hyena(hyena_query, hyena_key, hyena_value, conv_filter, skip_gain):
    product = (hyena_key.astype(jnp.float32) * hyena_value.astype(jnp.float32)).astype(jnp.bfloat16)
    length = conv_filter.shape[1]
    tokens_here, feature_width = product.shape
    blocks = tokens_here // length
    previous = shifted(product[tokens_here - length :], "ctx", 1)
    widened = product.astype(jnp.float32)
    earlier = jnp.concatenate([previous, product[: tokens_here - length]], axis=0)
    convolved = local_conv(
        product.reshape(blocks, length, feature_width),
        earlier.reshape(blocks, length, feature_width),
        conv_filter,
    )
    return (hyena_query.astype(jnp.float32) * (convolved + skip_gain[None, :] * widened)).astype(
        jnp.bfloat16
    )


def chip_route(step):
    route = []
    for source in range(2 * CHIPS):
        y, x, core = source // 4, source // 2 % 2, source % 2
        target = ((y + step // 2) % CHIPS_Y * 2 + (x + step) % 2) * 2 + core
        route.append((source, target))
    return route


CORE_GROUPS = [list(range(core, 2 * CHIPS, 2)) for core in range(2)]
CORE_ROUTE = [(i, i ^ 1) for i in range(2 * CHIPS)]


def ring_route(step):
    return [(i, i // RING * RING + (i + step) % RING) for i in range(2 * RING)]


PAIR_ROUTE = [(i, (i + RING) % (2 * RING)) for i in range(2 * RING)]


def ahead(y, x, step):
    return ((y + step // 2) & 3) * 2 + ((x + step) & 1)


def behind(y, x, step):
    return ((y - step // 2) & 3) * 2 + ((x - step) & 1)


def split_kernel(q_ref, k_ref, v_ref, out_ref):
    rows = q_ref.shape[0]
    out_ref[0, :rows, :] = k_ref[...]
    out_ref[0, rows : 2 * rows, :] = v_ref[...]
    out_ref[0, 2 * rows :, :] = q_ref[...]


def split_heads(query_rows, key_rows, value_rows):
    rows = query_rows.shape[0]
    spec = pl.BlockSpec((rows, HEAD_DIM), lambda head: (0, head))
    return pl.pallas_call(
        split_kernel,
        grid=(CHIPS,),
        out_shape=jax.ShapeDtypeStruct((CHIPS, 3 * rows, HEAD_DIM), jnp.bfloat16),
        in_specs=[spec] * 3,
        out_specs=pl.BlockSpec((1, 3 * rows, HEAD_DIM), lambda head: (head, 0, 0)),
        name="split_heads",
    )(query_rows, key_rows, value_rows)


def attention_kernel(place, own, other, *refs):
    outs = refs[:CHIPS]
    keys, values, top, total = refs[CHIPS:]
    y, x, core = place[0], place[1], place[2]
    step = pl.program_id(0)
    rows = top.shape[0]

    @pl.when(step == 0)
    def _():
        ones = jnp.ones((2 * rows, HEAD_DIM), jnp.bfloat16)
        for i in range(CHIPS):
            keys[i, :, :rows] = own[i, :rows, :].T
            keys[i, :, rows:] = other[i, :rows, :].T
            values[i, :rows, :HEAD_DIM] = own[i, rows : 2 * rows, :]
            values[i, rows:, :HEAD_DIM] = other[i, rows:, :]
            values[i, :, HEAD_DIM:] = ones

    top[...] = jnp.full_like(top, NEGATIVE)
    total[...] = jnp.zeros_like(total)
    chip = ahead(y, x, step)

    def update(slot, first, width, masked):
        scores = jnp.dot(
            own[chip, 2 * rows :, :],
            keys[slot, :, first : first + width],
            preferred_element_type=jnp.float32,
        )
        if masked:
            row = lax.broadcasted_iota(jnp.int32, scores.shape, 0)
            column = lax.broadcasted_iota(jnp.int32, scores.shape, 1)
            scores = jnp.where(column <= row, scores, NEGATIVE)
        old = top[...]
        new = jnp.maximum(old, jnp.max(scores, axis=1, keepdims=True))
        keep = jnp.exp2((old - new) * EXP_SCALE)
        spread = jnp.concatenate([new] * (width // HEAD_DIM), axis=1)
        weights = jnp.exp2((scores - spread) * EXP_SCALE).astype(jnp.bfloat16)
        total[...] = total[...] * jnp.concatenate([keep, keep], axis=1) + jnp.dot(
            weights, values[slot, first : first + width, :], preferred_element_type=jnp.float32
        )
        top[...] = new

    def full_step(j, unused):
        update(j, 0, 2 * rows, False)
        return unused

    lax.fori_loop(0, chip, full_step, 0)
    update(chip, 0, rows, True)

    @pl.when(core == 1)
    def _():
        update(chip, rows, rows, False)

    result = (total[:, :HEAD_DIM] / total[:, HEAD_DIM:]).astype(jnp.bfloat16)
    for i in range(CHIPS):

        @pl.when(step == i)
        def _(i=i):
            outs[i][...] = result


def attention(place, own, other):
    rows = own.shape[1] // 3
    return pl.pallas_call(
        attention_kernel,
        grid=(CHIPS,),
        out_shape=[jax.ShapeDtypeStruct((rows, HEAD_DIM), jnp.bfloat16)] * CHIPS,
        in_specs=[SMEM_SPEC, VMEM_SPEC, VMEM_SPEC],
        out_specs=[VMEM_SPEC] * CHIPS,
        scratch_shapes=[
            VMEM((CHIPS, HEAD_DIM, 2 * rows), jnp.bfloat16),
            VMEM((CHIPS, 2 * rows, 2 * HEAD_DIM), jnp.bfloat16),
            VMEM((rows, HEAD_DIM), jnp.float32),
            VMEM((rows, 2 * HEAD_DIM), jnp.float32),
        ],
        cost_estimate=pl.CostEstimate(
            flops=12_000_000_000, bytes_accessed=6_000_000, transcendentals=10_000_000
        ),
        name="attention",
    )(place, own, other)


def join_kernel(place, *refs):
    y, x = place[0], place[1]
    joined = refs[CHIPS]
    for step in range(CHIPS):
        column = pl.multiple_of(behind(y, x, step) * HEAD_DIM, HEAD_DIM)
        joined[:, pl.ds(column, HEAD_DIM)] = refs[step][...]


def join_heads(place, pieces):
    rows = pieces[0].shape[0]
    return pl.pallas_call(
        join_kernel,
        out_shape=jax.ShapeDtypeStruct((rows, CHIPS * HEAD_DIM), jnp.bfloat16),
        in_specs=[SMEM_SPEC] + [VMEM_SPEC] * CHIPS,
        out_specs=VMEM_SPEC,
        name="join_heads",
    )(place, *pieces)


def project(place, wanted, out_weight, attended):
    rows, features = attended.shape
    share = out_weight.shape[0] // (4 * RING)

    def weight_block(step, place):
        index = jnp.int32(0)
        for i, (x_off, z_off, half) in enumerate(wanted):
            row = ((((place[3] + x_off) & 1) * RING + ((place[4] + z_off) & 3)) * 2) + half
            index = jnp.where(step == i, row, index)
        return (index, 0)

    def kernel(place, weight_ref, attended_ref, *outs):
        piece = lax.dot_general(
            weight_ref[...],
            attended_ref[...],
            (((1,), (1,)), ((), ())),
            preferred_element_type=jnp.float32,
        ).astype(jnp.bfloat16)
        for i in range(len(wanted)):

            @pl.when(pl.program_id(0) == i)
            def _(i=i):
                outs[i][...] = piece

    count = len(wanted)
    return pl.pallas_call(
        kernel,
        grid_spec=pltpu.PrefetchScalarGridSpec(
            num_scalar_prefetch=1,
            grid=(count,),
            in_specs=[
                pl.BlockSpec((share, features), weight_block),
                pl.BlockSpec((rows, features), lambda step, place: (0, 0)),
            ],
            out_specs=[pl.BlockSpec((share, rows), lambda step, place: (0, 0))] * count,
        ),
        out_shape=[jax.ShapeDtypeStruct((share, rows), jnp.bfloat16)] * count,
        cost_estimate=pl.CostEstimate(
            flops=2 * share * rows * features * count,
            bytes_accessed=share * features * 2 * count,
            transcendentals=0,
        ),
        name="project",
    )(place, out_weight, attended)


def added(*pieces):
    return sum(piece.astype(jnp.float32) for piece in pieces)


def local_step(
    hyena_query,
    hyena_key,
    hyena_value,
    conv_filter,
    skip_gain,
    query_rows,
    key_rows,
    value_rows,
    out_weight,
):
    ctx = lax.axis_index("ctx")
    tp = lax.axis_index("tp")
    place = jnp.stack([ctx // 4, ctx // 2 % 2, ctx % 2, tp // RING, tp % RING]).astype(jnp.int32)

    rows = query_rows.shape[0]
    pieces = split_heads(query_rows, key_rows, value_rows)
    own = lax.all_to_all(pieces, "ctx", 0, 0, axis_index_groups=CORE_GROUPS, tiled=True)
    hyena_out = hyena(hyena_query, hyena_key, hyena_value, conv_filter, skip_gain)
    other = lax.ppermute(own[:, : 2 * rows], "ctx", CORE_ROUTE)
    outs = attention(place, own, other)
    back = [outs[0]] + [
        lax.ppermute(outs[step], "ctx", chip_route(step)) for step in range(1, CHIPS)
    ]
    attended = join_heads(place, back)

    kept = []
    handed = None
    for x_off in (1, 0):

        def sent(block, step):
            return lax.ppermute(block, "tp", ring_route(step))

        far = project(place, [(x_off, 2, 0), (x_off, 2, 1)], out_weight, attended)
        near = project(
            place,
            [
                (x_off, 1, 1),
                (x_off, 3, 0),
                (x_off, 1, 0),
                (x_off, 3, 1),
                (x_off, 0, 0),
                (x_off, 0, 1),
            ],
            out_weight,
            attended,
        )
        from_below = sent(far[0], 1)
        from_above = sent(far[1], -1)
        below_1 = sent(near[0], 1)
        above_0 = sent(near[1], -1)
        up = added(near[2], from_below).astype(jnp.bfloat16)
        down = added(near[3], from_above).astype(jnp.bfloat16)
        below_0 = sent(up, 1)
        above_1 = sent(down, -1)
        first = added(near[4], below_0, above_0)
        second = added(near[5], below_1, above_1)
        if x_off == 1:
            handed = [
                lax.ppermute(part.astype(jnp.bfloat16), "tp", PAIR_ROUTE)
                for part in (first, second)
            ]
        else:
            kept = [first, second]
    attention_out = jnp.concatenate(
        [(kept[i] + handed[i].astype(jnp.float32)).astype(jnp.bfloat16) for i in range(2)], axis=0
    )
    return (hyena_out, attention_out)


def solution(mesh):
    in_specs = (
        P("ctx", "tp"),
        P("ctx", "tp"),
        P("ctx", "tp"),
        P("tp", None),
        P("tp"),
        P("ctx", "tp"),
        P("ctx", "tp"),
        P("ctx", "tp"),
        P(None, "tp"),
    )
    out_specs = (P("ctx", "tp"), P("tp", "ctx"))
    return jax.shard_map(local_step, mesh=mesh, in_specs=in_specs, out_specs=out_specs, check_vma=False)
```

```python
import jax
import jax.numpy as jnp
from jax import lax
from jax.experimental import pallas as pl
from jax.experimental.pallas import tpu as pltpu
from jax.sharding import PartitionSpec as P

HEAD_DIM = 128
CHIPS_Y = 4
CHIPS = 8
RING = 4
NEGATIVE = -1e30
EXP_SCALE = HEAD_DIM ** (-0.5) * 1.4426950408889634


VMEM = pltpu.VMEM
SMEM_SPEC = pl.BlockSpec(memory_space=pltpu.SMEM)
VMEM_SPEC = pl.BlockSpec(memory_space=pltpu.VMEM)


def shifted(block, axis, distance):
    devices = range(lax.axis_size(axis))
    route = [(i - distance, i) for i in devices if i - distance in devices]
    return lax.ppermute(block, axis, route)


LANES = 128


def hyena_kernel(query, key, value, before, taps, gain, out, product):
    length = before.shape[0]
    rows = query.shape[0]
    groups = taps.shape[0]
    product[:length, :] = before[...]
    product[length:, :] = (
        key[...].astype(jnp.float32) * value[...].astype(jnp.float32)
    ).astype(jnp.bfloat16)
    tables = []
    for group in range(groups):
        row = jnp.broadcast_to(taps[group : group + 1, :], (length, 2 * length))
        tables.append(pltpu.roll(row, 0, 1, stride=1, stride_axis=0).astype(jnp.bfloat16))
    table = jnp.concatenate(tables, axis=0)
    lane_group = lax.broadcasted_iota(jnp.int32, (length, LANES), 1) // (LANES // groups)
    for first in range(0, rows, length):
        spread = jnp.dot(
            table, product[first : first + 2 * length, :], preferred_element_type=jnp.float32
        )
        convolved = spread[:length]
        for group in range(1, groups):
            convolved = jnp.where(
                lane_group == group, spread[group * length : (group + 1) * length], convolved
            )
        here = slice(first, first + length)
        current = product[first + length : first + 2 * length, :].astype(jnp.float32)
        out[here, :] = (
            query[here, :].astype(jnp.float32) * (convolved + gain[...] * current)
        ).astype(jnp.bfloat16)


def hyena(hyena_query, hyena_key, hyena_value, before, conv_filter, skip_gain):
    rows, width = hyena_query.shape
    groups, length = conv_filter.shape
    share = groups * LANES // width
    taps = jnp.concatenate(
        [
            jnp.zeros((groups, 1), jnp.float32),
            conv_filter[:, ::-1].astype(jnp.float32),
            jnp.zeros((groups, length - 1), jnp.float32),
        ],
        axis=1,
    )

    def columns(height):
        return pl.BlockSpec((height, LANES), lambda i: (0, i))

    return pl.pallas_call(
        hyena_kernel,
        grid=(width // LANES,),
        out_shape=jax.ShapeDtypeStruct((rows, width), jnp.bfloat16),
        in_specs=[
            columns(rows),
            columns(rows),
            columns(rows),
            columns(length),
            pl.BlockSpec((share, 2 * length), lambda i: (i, 0)),
            columns(1),
        ],
        out_specs=columns(rows),
        scratch_shapes=[VMEM((rows + length, LANES), jnp.bfloat16)],
        cost_estimate=pl.CostEstimate(
            flops=3_000_000_000, bytes_accessed=3_000_000, transcendentals=0
        ),
        name="hyena",
    )(hyena_query, hyena_key, hyena_value, before, taps, skip_gain[None, :])


def chip_route(step):
    route = []
    for source in range(2 * CHIPS):
        y, x, core = source // 4, source // 2 % 2, source % 2
        target = ((y + step // 2) % CHIPS_Y * 2 + (x + step) % 2) * 2 + core
        route.append((source, target))
    return route


CORE_GROUPS = [list(range(core, 2 * CHIPS, 2)) for core in range(2)]
CORE_ROUTE = [(i, i ^ 1) for i in range(2 * CHIPS)]


def ring_route(step):
    return [(i, i // RING * RING + (i + step) % RING) for i in range(2 * RING)]


PAIR_ROUTE = [(i, (i + RING) % (2 * RING)) for i in range(2 * RING)]


def ahead(y, x, step):
    return ((y + step // 2) & 3) * 2 + ((x + step) & 1)


def behind(y, x, step):
    return ((y - step // 2) & 3) * 2 + ((x - step) & 1)


def split_kernel(q_ref, k_ref, v_ref, out_ref):
    rows = q_ref.shape[0]
    for head in range(out_ref.shape[0]):
        columns = slice(head * HEAD_DIM, (head + 1) * HEAD_DIM)
        out_ref[head, :rows, :] = k_ref[:, columns]
        out_ref[head, rows : 2 * rows, :] = v_ref[:, columns]
        out_ref[head, 2 * rows :, :] = q_ref[:, columns]


def split_heads(query_rows, key_rows, value_rows):
    rows = query_rows.shape[0]
    at_once = 2
    spec = pl.BlockSpec((rows, at_once * HEAD_DIM), lambda step: (0, step))
    return pl.pallas_call(
        split_kernel,
        grid=(CHIPS // at_once,),
        out_shape=jax.ShapeDtypeStruct((CHIPS, 3 * rows, HEAD_DIM), jnp.bfloat16),
        in_specs=[spec] * 3,
        out_specs=pl.BlockSpec((at_once, 3 * rows, HEAD_DIM), lambda step: (step, 0, 0)),
        name="split_heads",
    )(query_rows, key_rows, value_rows)


def attention_kernel(place, own, other, *refs):
    outs = refs[:CHIPS]
    keys, values, top, total, even, odd = refs[CHIPS:]
    y, x, core = place[0], place[1], place[2]
    step = pl.program_id(0)
    rows = top.shape[0]

    @pl.when(step == 0)
    def _():
        ones = jnp.ones((2 * rows, HEAD_DIM), jnp.bfloat16)
        for i in range(CHIPS):
            keys[i, :, :rows] = own[i, :rows, :].T
            keys[i, :, rows:] = other[i, :rows, :].T
            values[i, :rows, :HEAD_DIM] = own[i, rows : 2 * rows, :]
            values[i, rows:, :HEAD_DIM] = other[i, rows:, :]
            values[i, :, HEAD_DIM:] = ones

    top[...] = jnp.full_like(top, NEGATIVE)
    total[...] = jnp.zeros_like(total)
    chip = ahead(y, x, step)

    def score(held, block):
        held[...] = jnp.dot(
            own[chip, 2 * rows :, :], keys[block], preferred_element_type=jnp.float32
        )

    def weigh(held, block, masked):
        scores = held[...]
        if masked:
            row = lax.broadcasted_iota(jnp.int32, scores.shape, 0)
            column = lax.broadcasted_iota(jnp.int32, scores.shape, 1)
            limit = rows + core * rows
            allowed = (column <= row) | ((column >= rows) & (column < limit))
            scores = jnp.where(allowed, scores, NEGATIVE)
        old = top[...]
        new = jnp.maximum(old, jnp.max(scores, axis=1, keepdims=True))
        keep = jnp.exp2((old - new) * EXP_SCALE)
        spread = jnp.concatenate([new] * (2 * rows // HEAD_DIM), axis=1)
        weights = jnp.exp2((scores - spread) * EXP_SCALE).astype(jnp.bfloat16)
        total[...] = total[...] * jnp.concatenate([keep, keep], axis=1) + jnp.dot(
            weights, values[block], preferred_element_type=jnp.float32
        )
        top[...] = new

    score(even, 0)

    def two_blocks(pair, unused):
        score(odd, 2 * pair + 1)
        weigh(even, 2 * pair, False)
        score(even, 2 * pair + 2)
        weigh(odd, 2 * pair + 1, False)
        return unused

    lax.fori_loop(0, chip >> 1, two_blocks, 0)

    @pl.when((chip & 1) == 0)
    def _():
        weigh(even, chip, True)

    @pl.when((chip & 1) == 1)
    def _():
        score(odd, chip)
        weigh(even, chip - 1, False)
        weigh(odd, chip, True)

    result = (total[:, :HEAD_DIM] / total[:, HEAD_DIM:]).astype(jnp.bfloat16)
    for i in range(CHIPS):

        @pl.when(step == i)
        def _(i=i):
            outs[i][...] = result


def attention(place, own, other):
    rows = own.shape[1] // 3
    return pl.pallas_call(
        attention_kernel,
        grid=(CHIPS,),
        out_shape=[jax.ShapeDtypeStruct((rows, HEAD_DIM), jnp.bfloat16)] * CHIPS,
        in_specs=[SMEM_SPEC, VMEM_SPEC, VMEM_SPEC],
        out_specs=[VMEM_SPEC] * CHIPS,
        scratch_shapes=[
            VMEM((CHIPS, HEAD_DIM, 2 * rows), jnp.bfloat16),
            VMEM((CHIPS, 2 * rows, 2 * HEAD_DIM), jnp.bfloat16),
            VMEM((rows, HEAD_DIM), jnp.float32),
            VMEM((rows, 2 * HEAD_DIM), jnp.float32),
            VMEM((rows, 2 * rows), jnp.float32),
            VMEM((rows, 2 * rows), jnp.float32),
        ],
        cost_estimate=pl.CostEstimate(
            flops=12_000_000_000, bytes_accessed=6_000_000, transcendentals=10_000_000
        ),
        name="attention",
    )(place, own, other)


def join_kernel(place, *refs):
    y, x = place[0], place[1]
    joined = refs[CHIPS]
    for step in range(CHIPS):
        column = pl.multiple_of(behind(y, x, step) * HEAD_DIM, HEAD_DIM)
        joined[:, pl.ds(column, HEAD_DIM)] = refs[step][...]


def join_heads(place, pieces):
    rows = pieces[0].shape[0]
    return pl.pallas_call(
        join_kernel,
        out_shape=jax.ShapeDtypeStruct((rows, CHIPS * HEAD_DIM), jnp.bfloat16),
        in_specs=[SMEM_SPEC] + [VMEM_SPEC] * CHIPS,
        out_specs=VMEM_SPEC,
        name="join_heads",
    )(place, *pieces)


def project(place, wanted, out_weight, attended):
    rows, features = attended.shape
    share = out_weight.shape[0] // (2 * RING)
    count = len(wanted)

    def weight_block(step, place):
        index = jnp.int32(0)
        for i, (x_off, z_off) in enumerate(wanted):
            block = ((place[3] + x_off) & 1) * RING + ((place[4] + z_off) & 3)
            index = jnp.where(step == i, block, index)
        return (index, 0)

    def kernel(place, weight_ref, attended_ref, *outs):
        piece = lax.dot_general(
            attended_ref[...],
            weight_ref[...],
            (((1,), (1,)), ((), ())),
            preferred_element_type=jnp.float32,
        )
        piece = piece.astype(jnp.bfloat16).T
        for i in range(count):

            @pl.when(pl.program_id(0) == i)
            def _(i=i):
                outs[2 * i][...] = piece[: share // 2]
                outs[2 * i + 1][...] = piece[share // 2 :]

    half = pl.BlockSpec((share // 2, rows), lambda step, place: (0, 0))
    return pl.pallas_call(
        kernel,
        grid_spec=pltpu.PrefetchScalarGridSpec(
            num_scalar_prefetch=1,
            grid=(count,),
            in_specs=[
                pl.BlockSpec((share, features), weight_block),
                pl.BlockSpec((rows, features), lambda step, place: (0, 0)),
            ],
            out_specs=[half] * (2 * count),
        ),
        out_shape=[jax.ShapeDtypeStruct((share // 2, rows), jnp.bfloat16)] * (2 * count),
        cost_estimate=pl.CostEstimate(
            flops=2 * share * rows * features * count,
            bytes_accessed=share * features * 2 * count,
            transcendentals=0,
        ),
        name="project",
    )(place, out_weight, attended)


def added(*pieces):
    return sum(piece.astype(jnp.float32) for piece in pieces)


def local_step(
    hyena_query,
    hyena_key,
    hyena_value,
    conv_filter,
    skip_gain,
    query_rows,
    key_rows,
    value_rows,
    out_weight,
):
    ctx = lax.axis_index("ctx")
    tp = lax.axis_index("tp")
    place = jnp.stack([ctx // 4, ctx // 2 % 2, ctx % 2, tp // RING, tp % RING]).astype(jnp.int32)

    rows = query_rows.shape[0]
    length = conv_filter.shape[1]
    tail = (
        hyena_key[rows - length :].astype(jnp.float32)
        * hyena_value[rows - length :].astype(jnp.float32)
    ).astype(jnp.bfloat16)
    before = shifted(tail, "ctx", 1)
    pieces = split_heads(query_rows, key_rows, value_rows)
    own = lax.all_to_all(pieces, "ctx", 0, 0, axis_index_groups=CORE_GROUPS, tiled=True)
    hyena_out = hyena(
        hyena_query, hyena_key, hyena_value, before, conv_filter, skip_gain
    )
    other = lax.ppermute(own[:, : 2 * rows], "ctx", CORE_ROUTE)
    outs = attention(place, own, other)
    back = [outs[0]] + [
        lax.ppermute(outs[step], "ctx", chip_route(step)) for step in range(1, CHIPS)
    ]
    attended = join_heads(place, back)

    kept = []
    handed = None
    for x_off in (1, 0):

        def sent(block, step):
            return lax.ppermute(block, "tp", ring_route(step))

        far = project(place, [(x_off, 2)], out_weight, attended)
        near = project(place, [(x_off, 1), (x_off, 3), (x_off, 0)], out_weight, attended)
        from_below = sent(far[0], 1)
        from_above = sent(far[1], -1)
        below_1 = sent(near[1], 1)
        above_0 = sent(near[2], -1)
        up = added(near[0], from_below).astype(jnp.bfloat16)
        down = added(near[3], from_above).astype(jnp.bfloat16)
        below_0 = sent(up, 1)
        above_1 = sent(down, -1)
        first = added(near[4], below_0, above_0)
        second = added(near[5], below_1, above_1)
        if x_off == 1:
            handed = [
                lax.ppermute(part.astype(jnp.bfloat16), "tp", PAIR_ROUTE)
                for part in (first, second)
            ]
        else:
            kept = [first, second]
    attention_out = jnp.concatenate(
        [(kept[i] + handed[i].astype(jnp.float32)).astype(jnp.bfloat16) for i in range(2)], axis=0
    )
    return (hyena_out, attention_out)


def solution(mesh):
    in_specs = (
        P("ctx", "tp"),
        P("ctx", "tp"),
        P("ctx", "tp"),
        P("tp", None),
        P("tp"),
        P("ctx", "tp"),
        P("ctx", "tp"),
        P("ctx", "tp"),
        P(None, "tp"),
    )
    out_specs = (P("ctx", "tp"), P("tp", "ctx"))
    return jax.shard_map(local_step, mesh=mesh, in_specs=in_specs, out_specs=out_specs, check_vma=False)
```

```python
import jax
import jax.numpy as jnp
from jax import lax
from jax.experimental import pallas as pl
from jax.experimental.pallas import tpu as pltpu
from jax.sharding import PartitionSpec as P

HEAD_DIM = 128
CHIPS_Y = 4
CHIPS = 8
RING = 4
NEGATIVE = -1e30
EXP_SCALE = HEAD_DIM ** (-0.5) * 1.4426950408889634


VMEM = pltpu.VMEM
SMEM_SPEC = pl.BlockSpec(memory_space=pltpu.SMEM)
VMEM_SPEC = pl.BlockSpec(memory_space=pltpu.VMEM)


def shifted(block, axis, distance):
    devices = range(lax.axis_size(axis))
    route = [(i - distance, i) for i in devices if i - distance in devices]
    return lax.ppermute(block, axis, route)


LANES = 128


def hyena_kernel(query, key, value, before, taps, gain, out, product):
    length = before.shape[0]
    rows = query.shape[0]
    groups = taps.shape[0]
    product[:length, :] = before[...]
    product[length:, :] = (
        key[...].astype(jnp.float32) * value[...].astype(jnp.float32)
    ).astype(jnp.bfloat16)
    tables = []
    for group in range(groups):
        row = jnp.broadcast_to(taps[group : group + 1, :], (length, 2 * length))
        tables.append(pltpu.roll(row, 0, 1, stride=1, stride_axis=0).astype(jnp.bfloat16))
    table = jnp.concatenate(tables, axis=0)
    lane_group = lax.broadcasted_iota(jnp.int32, (length, LANES), 1) // (LANES // groups)
    for first in range(0, rows, length):
        spread = jnp.dot(
            table, product[first : first + 2 * length, :], preferred_element_type=jnp.float32
        )
        convolved = spread[:length]
        for group in range(1, groups):
            convolved = jnp.where(
                lane_group == group, spread[group * length : (group + 1) * length], convolved
            )
        here = slice(first, first + length)
        current = product[first + length : first + 2 * length, :].astype(jnp.float32)
        out[here, :] = (
            query[here, :].astype(jnp.float32) * (convolved + gain[...] * current)
        ).astype(jnp.bfloat16)


def hyena(hyena_query, hyena_key, hyena_value, before, conv_filter, skip_gain):
    rows, width = hyena_query.shape
    groups, length = conv_filter.shape
    share = groups * LANES // width
    taps = jnp.concatenate(
        [
            jnp.zeros((groups, 1), jnp.float32),
            conv_filter[:, ::-1].astype(jnp.float32),
            jnp.zeros((groups, length - 1), jnp.float32),
        ],
        axis=1,
    )

    def columns(height):
        return pl.BlockSpec((height, LANES), lambda i: (0, i))

    return pl.pallas_call(
        hyena_kernel,
        grid=(width // LANES,),
        out_shape=jax.ShapeDtypeStruct((rows, width), jnp.bfloat16),
        in_specs=[
            columns(rows),
            columns(rows),
            columns(rows),
            columns(length),
            pl.BlockSpec((share, 2 * length), lambda i: (i, 0)),
            columns(1),
        ],
        out_specs=columns(rows),
        scratch_shapes=[VMEM((rows + length, LANES), jnp.bfloat16)],
        cost_estimate=pl.CostEstimate(
            flops=3_000_000_000, bytes_accessed=3_000_000, transcendentals=0
        ),
        name="hyena",
    )(hyena_query, hyena_key, hyena_value, before, taps, skip_gain[None, :])


def chip_route(step):
    route = []
    for source in range(2 * CHIPS):
        y, x, core = source // 4, source // 2 % 2, source % 2
        target = ((y + step // 2) % CHIPS_Y * 2 + (x + step) % 2) * 2 + core
        route.append((source, target))
    return route


CORE_GROUPS = [list(range(core, 2 * CHIPS, 2)) for core in range(2)]
CORE_ROUTE = [(i, i ^ 1) for i in range(2 * CHIPS)]


def ring_route(step):
    return [(i, i // RING * RING + (i + step) % RING) for i in range(2 * RING)]


PAIR_ROUTE = [(i, (i + RING) % (2 * RING)) for i in range(2 * RING)]


def ahead(y, x, step):
    return ((y + step // 2) & 3) * 2 + ((x + step) & 1)


def behind(y, x, step):
    return ((y - step // 2) & 3) * 2 + ((x - step) & 1)


def split_kernel(*refs):
    out_ref = refs[-1]
    rows = refs[0].shape[0]
    for head in range(out_ref.shape[0]):
        columns = slice(head * HEAD_DIM, (head + 1) * HEAD_DIM)
        for i, ref in enumerate(refs[:-1]):
            out_ref[head, i * rows : (i + 1) * rows, :] = ref[:, columns]


def split_heads(*arrays):
    rows = arrays[0].shape[0]
    at_once = 4
    spec = pl.BlockSpec((rows, at_once * HEAD_DIM), lambda step: (0, step))
    tall = len(arrays) * rows
    return pl.pallas_call(
        split_kernel,
        grid=(CHIPS // at_once,),
        out_shape=jax.ShapeDtypeStruct((CHIPS, tall, HEAD_DIM), jnp.bfloat16),
        in_specs=[spec] * len(arrays),
        out_specs=pl.BlockSpec((at_once, tall, HEAD_DIM), lambda step: (step, 0, 0)),
        name="split_heads",
    )(*arrays)


def split_queries_kernel(place, query_ref, *outs):
    for step in range(CHIPS):
        column = pl.multiple_of(ahead(place[0], place[1], step) * HEAD_DIM, HEAD_DIM)
        outs[step][...] = query_ref[:, pl.ds(column, HEAD_DIM)]


def split_queries(place, query_rows):
    rows = query_rows.shape[0]
    return pl.pallas_call(
        split_queries_kernel,
        out_shape=[jax.ShapeDtypeStruct((rows, HEAD_DIM), jnp.bfloat16)] * CHIPS,
        in_specs=[SMEM_SPEC, VMEM_SPEC],
        out_specs=[VMEM_SPEC] * CHIPS,
        name="split_queries",
    )(place, query_rows)


def same_place(place):
    def kernel(place, out):
        for i in range(place.shape[0]):
            out[i] = place[i]

    return pl.pallas_call(
        kernel,
        out_shape=jax.ShapeDtypeStruct(place.shape, place.dtype),
        in_specs=[SMEM_SPEC],
        out_specs=SMEM_SPEC,
        name="same_place",
    )(place)


def attention_kernel(place, own, other, *refs):
    queries = refs[:CHIPS]
    outs = refs[CHIPS : 2 * CHIPS]
    now, keys, values, top, total, even, odd = refs[2 * CHIPS :]
    y, x, core = place[0], place[1], place[2]
    step = pl.program_id(0)
    rows = top.shape[0]

    @pl.when(step == 0)
    def _():
        ones = jnp.ones((2 * rows, HEAD_DIM), jnp.bfloat16)
        for i in range(CHIPS):
            keys[i, :, :rows] = own[i, :rows, :].T
            keys[i, :, rows:] = other[i, :rows, :].T
            values[i, :rows, :HEAD_DIM] = own[i, rows:, :]
            values[i, rows:, :HEAD_DIM] = other[i, rows:, :]
            values[i, :, HEAD_DIM:] = ones

    for i in range(CHIPS):

        @pl.when(step == i)
        def _(i=i):
            now[...] = queries[i][...]

    top[...] = jnp.full_like(top, NEGATIVE)
    total[...] = jnp.zeros_like(total)
    chip = ahead(y, x, step)

    def score(held, block):
        held[...] = jnp.dot(now[...], keys[block], preferred_element_type=jnp.float32)

    def weigh(held, block, masked):
        scores = held[...]
        if masked:
            row = lax.broadcasted_iota(jnp.int32, scores.shape, 0)
            column = lax.broadcasted_iota(jnp.int32, scores.shape, 1)
            limit = rows + core * rows
            allowed = (column <= row) | ((column >= rows) & (column < limit))
            scores = jnp.where(allowed, scores, NEGATIVE)
        old = top[...]
        new = jnp.maximum(old, jnp.max(scores, axis=1, keepdims=True))
        keep = jnp.exp2((old - new) * EXP_SCALE)
        spread = jnp.concatenate([new] * (2 * rows // HEAD_DIM), axis=1)
        weights = jnp.exp2((scores - spread) * EXP_SCALE).astype(jnp.bfloat16)
        total[...] = total[...] * jnp.concatenate([keep, keep], axis=1) + jnp.dot(
            weights, values[block], preferred_element_type=jnp.float32
        )
        top[...] = new

    score(even, 0)

    def two_blocks(pair, unused):
        score(odd, 2 * pair + 1)
        weigh(even, 2 * pair, False)
        score(even, 2 * pair + 2)
        weigh(odd, 2 * pair + 1, False)
        return unused

    lax.fori_loop(0, chip >> 1, two_blocks, 0)

    @pl.when((chip & 1) == 0)
    def _():
        weigh(even, chip, True)

    @pl.when((chip & 1) == 1)
    def _():
        score(odd, chip)
        weigh(even, chip - 1, False)
        weigh(odd, chip, True)

    result = (total[:, :HEAD_DIM] / total[:, HEAD_DIM:]).astype(jnp.bfloat16)
    for i in range(CHIPS):

        @pl.when(step == i)
        def _(i=i):
            outs[i][...] = result


def attention(place, queries, own, other):
    rows = queries[0].shape[0]
    return pl.pallas_call(
        attention_kernel,
        grid=(CHIPS,),
        out_shape=[jax.ShapeDtypeStruct((rows, HEAD_DIM), jnp.bfloat16)] * CHIPS,
        in_specs=[SMEM_SPEC] + [VMEM_SPEC] * (2 + CHIPS),
        out_specs=[VMEM_SPEC] * CHIPS,
        scratch_shapes=[
            VMEM((rows, HEAD_DIM), jnp.bfloat16),
            VMEM((CHIPS, HEAD_DIM, 2 * rows), jnp.bfloat16),
            VMEM((CHIPS, 2 * rows, 2 * HEAD_DIM), jnp.bfloat16),
            VMEM((rows, HEAD_DIM), jnp.float32),
            VMEM((rows, 2 * HEAD_DIM), jnp.float32),
            VMEM((rows, 2 * rows), jnp.float32),
            VMEM((rows, 2 * rows), jnp.float32),
        ],
        cost_estimate=pl.CostEstimate(
            flops=12_000_000_000, bytes_accessed=6_000_000, transcendentals=10_000_000
        ),
        name="attention",
    )(place, own, other, *queries)


def project_first(place, pieces, out_weight, x_off, z_off):
    rows = pieces[0].shape[0]
    share = out_weight.shape[0] // (2 * RING)
    features = out_weight.shape[1]

    def weight_block(step, place):
        return (((place[3] + x_off) & 1) * RING + ((place[4] + z_off) & 3), 0)

    def kernel(place, weight_ref, *refs):
        joined, lower, upper = refs[CHIPS:]
        for step in range(CHIPS):
            column = pl.multiple_of(behind(place[0], place[1], step) * HEAD_DIM, HEAD_DIM)
            joined[:, pl.ds(column, HEAD_DIM)] = refs[step][...]
        piece = lax.dot_general(
            joined[...],
            weight_ref[...],
            (((1,), (1,)), ((), ())),
            preferred_element_type=jnp.float32,
        )
        piece = piece.astype(jnp.bfloat16).T
        lower[...] = piece[: share // 2]
        upper[...] = piece[share // 2 :]

    def whole(height, width):
        return pl.BlockSpec((height, width), lambda step, place: (0, 0))

    return pl.pallas_call(
        kernel,
        grid_spec=pltpu.PrefetchScalarGridSpec(
            num_scalar_prefetch=1,
            grid=(1,),
            in_specs=[pl.BlockSpec((share, features), weight_block)]
            + [whole(rows, HEAD_DIM)] * CHIPS,
            out_specs=[whole(rows, features)] + [whole(share // 2, rows)] * 2,
        ),
        out_shape=[jax.ShapeDtypeStruct((rows, features), jnp.bfloat16)]
        + [jax.ShapeDtypeStruct((share // 2, rows), jnp.bfloat16)] * 2,
        cost_estimate=pl.CostEstimate(
            flops=2 * share * rows * features,
            bytes_accessed=share * features * 2,
            transcendentals=0,
        ),
        name="project_first",
    )(place, out_weight, *pieces)


def project(place, wanted, out_weight, attended):
    rows, features = attended.shape
    share = out_weight.shape[0] // (2 * RING)
    count = len(wanted)

    def weight_block(step, place):
        index = jnp.int32(0)
        for i, (x_off, z_off) in enumerate(wanted):
            block = ((place[3] + x_off) & 1) * RING + ((place[4] + z_off) & 3)
            index = jnp.where(step == i, block, index)
        return (index, 0)

    def kernel(place, weight_ref, attended_ref, *outs):
        piece = lax.dot_general(
            attended_ref[...],
            weight_ref[...],
            (((1,), (1,)), ((), ())),
            preferred_element_type=jnp.float32,
        )
        piece = piece.astype(jnp.bfloat16).T
        for i in range(count):

            @pl.when(pl.program_id(0) == i)
            def _(i=i):
                outs[2 * i][...] = piece[: share // 2]
                outs[2 * i + 1][...] = piece[share // 2 :]

    half = pl.BlockSpec((share // 2, rows), lambda step, place: (0, 0))
    return pl.pallas_call(
        kernel,
        grid_spec=pltpu.PrefetchScalarGridSpec(
            num_scalar_prefetch=1,
            grid=(count,),
            in_specs=[
                pl.BlockSpec((share, features), weight_block),
                pl.BlockSpec((rows, features), lambda step, place: (0, 0)),
            ],
            out_specs=[half] * (2 * count),
        ),
        out_shape=[jax.ShapeDtypeStruct((share // 2, rows), jnp.bfloat16)] * (2 * count),
        cost_estimate=pl.CostEstimate(
            flops=2 * share * rows * features * count,
            bytes_accessed=share * features * 2 * count,
            transcendentals=0,
        ),
        name="project",
    )(place, out_weight, attended)


def added(*pieces):
    return sum(piece.astype(jnp.float32) for piece in pieces)


def local_step(
    hyena_query,
    hyena_key,
    hyena_value,
    conv_filter,
    skip_gain,
    query_rows,
    key_rows,
    value_rows,
    out_weight,
):
    ctx = lax.axis_index("ctx")
    tp = lax.axis_index("tp")
    place = jnp.stack([ctx // 4, ctx // 2 % 2, ctx % 2, tp // RING, tp % RING])
    place = place.astype(jnp.int32)

    rows = query_rows.shape[0]
    length = conv_filter.shape[1]
    tail = (
        hyena_key[rows - length :].astype(jnp.float32)
        * hyena_value[rows - length :].astype(jnp.float32)
    ).astype(jnp.bfloat16)
    pieces = split_heads(key_rows, value_rows)
    own = lax.all_to_all(pieces, "ctx", 0, 0, axis_index_groups=CORE_GROUPS, tiled=True)
    before = shifted(tail, "ctx", 1)
    hyena_out = hyena(
        hyena_query, hyena_key, hyena_value, before, conv_filter, skip_gain
    )
    query_rows, hyena_out = lax.optimization_barrier((query_rows, hyena_out))
    asked = split_queries(place, query_rows)
    came = [asked[0]] + [
        lax.ppermute(asked[step], "ctx", chip_route(step)) for step in range(1, CHIPS)
    ]
    queries = [came[((-(i // 2)) % CHIPS_Y) * 2 + i % 2] for i in range(CHIPS)]
    place = same_place(place)
    other = lax.ppermute(own, "ctx", CORE_ROUTE)
    outs = attention(place, queries, own, other)
    back = [outs[0]] + [
        lax.ppermute(outs[step], "ctx", chip_route(step)) for step in range(1, CHIPS)
    ]
    kept = []
    handed = None
    for x_off in (1, 0):

        def sent(block, step):
            return lax.ppermute(block, "tp", ring_route(step))

        if x_off == 1:
            attended, *far = project_first(place, back, out_weight, x_off, 2)
        else:
            far = project(place, [(x_off, 2)], out_weight, attended)
        near = project(place, [(x_off, 1), (x_off, 3), (x_off, 0)], out_weight, attended)
        from_below = sent(far[0], 1)
        from_above = sent(far[1], -1)
        below_1 = sent(near[1], 1)
        above_0 = sent(near[2], -1)
        up = added(near[0], from_below).astype(jnp.bfloat16)
        down = added(near[3], from_above).astype(jnp.bfloat16)
        below_0 = sent(up, 1)
        above_1 = sent(down, -1)
        first = added(near[4], below_0, above_0)
        second = added(near[5], below_1, above_1)
        if x_off == 1:
            handed = [
                lax.ppermute(part.astype(jnp.bfloat16), "tp", PAIR_ROUTE)
                for part in (first, second)
            ]
        else:
            kept = [first, second]
    attention_out = jnp.concatenate(
        [(kept[i] + handed[i].astype(jnp.float32)).astype(jnp.bfloat16) for i in range(2)], axis=0
    )
    return (hyena_out, attention_out)


def solution(mesh):
    in_specs = (
        P("ctx", "tp"),
        P("ctx", "tp"),
        P("ctx", "tp"),
        P("tp", None),
        P("tp"),
        P("ctx", "tp"),
        P("ctx", "tp"),
        P("ctx", "tp"),
        P(None, "tp"),
    )
    out_specs = (P("ctx", "tp"), P("tp", "ctx"))
    return jax.shard_map(local_step, mesh=mesh, in_specs=in_specs, out_specs=out_specs, check_vma=False)
```

```python
import jax
import jax.numpy as jnp
from jax import lax
from jax.experimental import pallas as pl
from jax.experimental.pallas import tpu as pltpu
from jax.sharding import PartitionSpec as P

HEAD_DIM = 128
CHIPS_Y = 4
CHIPS = 8
RING = 4
NEGATIVE = -1e30
EXP_SCALE = HEAD_DIM ** (-0.5) * 1.4426950408889634


VMEM = pltpu.VMEM
SMEM_SPEC = pl.BlockSpec(memory_space=pltpu.SMEM)
VMEM_SPEC = pl.BlockSpec(memory_space=pltpu.VMEM)


def shifted(block, axis, distance):
    devices = range(lax.axis_size(axis))
    route = [(i - distance, i) for i in devices if i - distance in devices]
    return lax.ppermute(block, axis, route)


LANES = 128


def hyena_kernel(query, key, value, before, taps, gain, out, product):
    length = before.shape[0]
    rows = query.shape[0]
    groups = taps.shape[0]
    product[:length, :] = before[...]
    product[length:, :] = (
        key[...].astype(jnp.float32) * value[...].astype(jnp.float32)
    ).astype(jnp.bfloat16)
    tables = []
    for group in range(groups):
        row = jnp.broadcast_to(taps[group : group + 1, :], (length, 2 * length))
        tables.append(pltpu.roll(row, 0, 1, stride=1, stride_axis=0).astype(jnp.bfloat16))
    table = jnp.concatenate(tables, axis=0)
    lane_group = lax.broadcasted_iota(jnp.int32, (length, LANES), 1) // (LANES // groups)
    for first in range(0, rows, length):
        spread = jnp.dot(
            table, product[first : first + 2 * length, :], preferred_element_type=jnp.float32
        )
        convolved = spread[:length]
        for group in range(1, groups):
            convolved = jnp.where(
                lane_group == group, spread[group * length : (group + 1) * length], convolved
            )
        here = slice(first, first + length)
        current = product[first + length : first + 2 * length, :].astype(jnp.float32)
        out[here, :] = (
            query[here, :].astype(jnp.float32) * (convolved + gain[...] * current)
        ).astype(jnp.bfloat16)


def hyena(hyena_query, hyena_key, hyena_value, before, conv_filter, skip_gain):
    rows, width = hyena_query.shape
    groups, length = conv_filter.shape
    share = groups * LANES // width
    taps = jnp.concatenate(
        [
            jnp.zeros((groups, 1), jnp.float32),
            conv_filter[:, ::-1].astype(jnp.float32),
            jnp.zeros((groups, length - 1), jnp.float32),
        ],
        axis=1,
    )

    def columns(height):
        return pl.BlockSpec((height, LANES), lambda i: (0, i))

    return pl.pallas_call(
        hyena_kernel,
        grid=(width // LANES,),
        out_shape=jax.ShapeDtypeStruct((rows, width), jnp.bfloat16),
        in_specs=[
            columns(rows),
            columns(rows),
            columns(rows),
            columns(length),
            pl.BlockSpec((share, 2 * length), lambda i: (i, 0)),
            columns(1),
        ],
        out_specs=columns(rows),
        scratch_shapes=[VMEM((rows + length, LANES), jnp.bfloat16)],
        cost_estimate=pl.CostEstimate(
            flops=3_000_000_000, bytes_accessed=3_000_000, transcendentals=0
        ),
        name="hyena",
    )(hyena_query, hyena_key, hyena_value, before, taps, skip_gain[None, :])


def chip_route(step):
    route = []
    for source in range(2 * CHIPS):
        y, x, core = source // 4, source // 2 % 2, source % 2
        target = ((y + step // 2) % CHIPS_Y * 2 + (x + step) % 2) * 2 + core
        route.append((source, target))
    return route


CORE_GROUPS = [list(range(core, 2 * CHIPS, 2)) for core in range(2)]
CORE_ROUTE = [(i, i ^ 1) for i in range(2 * CHIPS)]


def ring_route(step):
    return [(i, i // RING * RING + (i + step) % RING) for i in range(2 * RING)]


PAIR_ROUTE = [(i, (i + RING) % (2 * RING)) for i in range(2 * RING)]


def ahead(y, x, step):
    return ((y + step // 2) & 3) * 2 + ((x + step) & 1)


def behind(y, x, step):
    return ((y - step // 2) & 3) * 2 + ((x - step) & 1)


def split_kernel(*refs):
    out_ref = refs[-1]
    rows = refs[0].shape[0]
    for head in range(out_ref.shape[0]):
        columns = slice(head * HEAD_DIM, (head + 1) * HEAD_DIM)
        for i, ref in enumerate(refs[:-1]):
            out_ref[head, i * rows : (i + 1) * rows, :] = ref[:, columns]


def split_heads(*arrays):
    rows = arrays[0].shape[0]
    at_once = 4
    spec = pl.BlockSpec((rows, at_once * HEAD_DIM), lambda step: (0, step))
    tall = len(arrays) * rows
    return pl.pallas_call(
        split_kernel,
        grid=(CHIPS // at_once,),
        out_shape=jax.ShapeDtypeStruct((CHIPS, tall, HEAD_DIM), jnp.bfloat16),
        in_specs=[spec] * len(arrays),
        out_specs=pl.BlockSpec((at_once, tall, HEAD_DIM), lambda step: (step, 0, 0)),
        name="split_heads",
    )(*arrays)


def attention_kernel(place, own, other, *refs):
    outs = refs[:CHIPS]
    keys, values, top, total, even, odd = refs[CHIPS:]
    y, x, core = place[0], place[1], place[2]
    step = pl.program_id(0)
    rows = top.shape[0]

    @pl.when(step == 0)
    def _():
        ones = jnp.ones((2 * rows, HEAD_DIM), jnp.bfloat16)
        for i in range(CHIPS):
            keys[i, :, :rows] = own[i, :rows, :].T
            keys[i, :, rows:] = other[i, :rows, :].T
            values[i, :rows, :HEAD_DIM] = own[i, rows : 2 * rows, :]
            values[i, rows:, :HEAD_DIM] = other[i, rows:, :]
            values[i, :, HEAD_DIM:] = ones

    top[...] = jnp.full_like(top, NEGATIVE)
    total[...] = jnp.zeros_like(total)
    chip = ahead(y, x, step)

    def score(held, block):
        held[...] = jnp.dot(
            own[chip, 2 * rows :, :], keys[block], preferred_element_type=jnp.float32
        )

    def weigh(held, block, masked):
        scores = held[...]
        if masked:
            row = lax.broadcasted_iota(jnp.int32, scores.shape, 0)
            column = lax.broadcasted_iota(jnp.int32, scores.shape, 1)
            limit = rows + core * rows
            allowed = (column <= row) | ((column >= rows) & (column < limit))
            scores = jnp.where(allowed, scores, NEGATIVE)
        old = top[...]
        new = jnp.maximum(old, jnp.max(scores, axis=1, keepdims=True))
        keep = jnp.exp2((old - new) * EXP_SCALE)
        spread = jnp.concatenate([new] * (2 * rows // HEAD_DIM), axis=1)
        weights = jnp.exp2((scores - spread) * EXP_SCALE).astype(jnp.bfloat16)
        total[...] = total[...] * jnp.concatenate([keep, keep], axis=1) + jnp.dot(
            weights, values[block], preferred_element_type=jnp.float32
        )
        top[...] = new

    score(even, 0)

    def two_blocks(pair, unused):
        score(odd, 2 * pair + 1)
        weigh(even, 2 * pair, False)
        score(even, 2 * pair + 2)
        weigh(odd, 2 * pair + 1, False)
        return unused

    lax.fori_loop(0, chip >> 1, two_blocks, 0)

    @pl.when((chip & 1) == 0)
    def _():
        weigh(even, chip, True)

    @pl.when((chip & 1) == 1)
    def _():
        score(odd, chip)
        weigh(even, chip - 1, False)
        weigh(odd, chip, True)

    result = (total[:, :HEAD_DIM] / total[:, HEAD_DIM:]).astype(jnp.bfloat16)
    for i in range(CHIPS):

        @pl.when(step == i)
        def _(i=i):
            outs[i][...] = result


def attention(place, own, other):
    rows = own.shape[1] // 3
    return pl.pallas_call(
        attention_kernel,
        grid=(CHIPS,),
        out_shape=[jax.ShapeDtypeStruct((rows, HEAD_DIM), jnp.bfloat16)] * CHIPS,
        in_specs=[SMEM_SPEC, VMEM_SPEC, VMEM_SPEC],
        out_specs=[VMEM_SPEC] * CHIPS,
        scratch_shapes=[
            VMEM((CHIPS, HEAD_DIM, 2 * rows), jnp.bfloat16),
            VMEM((CHIPS, 2 * rows, 2 * HEAD_DIM), jnp.bfloat16),
            VMEM((rows, HEAD_DIM), jnp.float32),
            VMEM((rows, 2 * HEAD_DIM), jnp.float32),
            VMEM((rows, 2 * rows), jnp.float32),
            VMEM((rows, 2 * rows), jnp.float32),
        ],
        cost_estimate=pl.CostEstimate(
            flops=12_000_000_000, bytes_accessed=6_000_000, transcendentals=10_000_000
        ),
        name="attention",
    )(place, own, other)


def project_first(place, pieces, out_weight, x_off, z_off):
    rows = pieces[0].shape[0]
    share = out_weight.shape[0] // (2 * RING)
    features = out_weight.shape[1]

    def weight_block(step, place):
        return (((place[3] + x_off) & 1) * RING + ((place[4] + z_off) & 3), 0)

    def kernel(place, weight_ref, *refs):
        joined, lower, upper = refs[CHIPS:]
        for step in range(CHIPS):
            column = pl.multiple_of(behind(place[0], place[1], step) * HEAD_DIM, HEAD_DIM)
            joined[:, pl.ds(column, HEAD_DIM)] = refs[step][...]
        piece = lax.dot_general(
            joined[...],
            weight_ref[...],
            (((1,), (1,)), ((), ())),
            preferred_element_type=jnp.float32,
        )
        piece = piece.astype(jnp.bfloat16).T
        lower[...] = piece[: share // 2]
        upper[...] = piece[share // 2 :]

    def whole(height, width):
        return pl.BlockSpec((height, width), lambda step, place: (0, 0))

    return pl.pallas_call(
        kernel,
        grid_spec=pltpu.PrefetchScalarGridSpec(
            num_scalar_prefetch=1,
            grid=(1,),
            in_specs=[pl.BlockSpec((share, features), weight_block)]
            + [whole(rows, HEAD_DIM)] * CHIPS,
            out_specs=[whole(rows, features)] + [whole(share // 2, rows)] * 2,
        ),
        out_shape=[jax.ShapeDtypeStruct((rows, features), jnp.bfloat16)]
        + [jax.ShapeDtypeStruct((share // 2, rows), jnp.bfloat16)] * 2,
        cost_estimate=pl.CostEstimate(
            flops=2 * share * rows * features,
            bytes_accessed=share * features * 2,
            transcendentals=0,
        ),
        name="project_first",
    )(place, out_weight, *pieces)


def project(place, wanted, out_weight, attended):
    rows, features = attended.shape
    share = out_weight.shape[0] // (2 * RING)
    count = len(wanted)

    def weight_block(step, place):
        index = jnp.int32(0)
        for i, (x_off, z_off) in enumerate(wanted):
            block = ((place[3] + x_off) & 1) * RING + ((place[4] + z_off) & 3)
            index = jnp.where(step == i, block, index)
        return (index, 0)

    def kernel(place, weight_ref, attended_ref, *outs):
        piece = lax.dot_general(
            attended_ref[...],
            weight_ref[...],
            (((1,), (1,)), ((), ())),
            preferred_element_type=jnp.float32,
        )
        piece = piece.astype(jnp.bfloat16).T
        for i in range(count):

            @pl.when(pl.program_id(0) == i)
            def _(i=i):
                outs[2 * i][...] = piece[: share // 2]
                outs[2 * i + 1][...] = piece[share // 2 :]

    half = pl.BlockSpec((share // 2, rows), lambda step, place: (0, 0))
    return pl.pallas_call(
        kernel,
        grid_spec=pltpu.PrefetchScalarGridSpec(
            num_scalar_prefetch=1,
            grid=(count,),
            in_specs=[
                pl.BlockSpec((share, features), weight_block),
                pl.BlockSpec((rows, features), lambda step, place: (0, 0)),
            ],
            out_specs=[half] * (2 * count),
        ),
        out_shape=[jax.ShapeDtypeStruct((share // 2, rows), jnp.bfloat16)] * (2 * count),
        cost_estimate=pl.CostEstimate(
            flops=2 * share * rows * features * count,
            bytes_accessed=share * features * 2 * count,
            transcendentals=0,
        ),
        name="project",
    )(place, out_weight, attended)


def added(*pieces):
    return sum(piece.astype(jnp.float32) for piece in pieces)


def local_step(
    hyena_query,
    hyena_key,
    hyena_value,
    conv_filter,
    skip_gain,
    query_rows,
    key_rows,
    value_rows,
    out_weight,
):
    ctx = lax.axis_index("ctx")
    tp = lax.axis_index("tp")
    place = jnp.stack([ctx // 4, ctx // 2 % 2, ctx % 2, tp // RING, tp % RING])
    place = place.astype(jnp.int32)

    rows = query_rows.shape[0]
    length = conv_filter.shape[1]
    tail = (
        hyena_key[rows - length :].astype(jnp.float32)
        * hyena_value[rows - length :].astype(jnp.float32)
    ).astype(jnp.bfloat16)
    pieces = split_heads(key_rows, value_rows, query_rows)
    own = lax.all_to_all(pieces, "ctx", 0, 0, axis_index_groups=CORE_GROUPS, tiled=True)
    before = shifted(tail, "ctx", 1)
    hyena_out = hyena(
        hyena_query, hyena_key, hyena_value, before, conv_filter, skip_gain
    )
    other = lax.ppermute(own[:, : 2 * rows], "ctx", CORE_ROUTE)
    outs = attention(place, own, other)
    back = [outs[0]] + [
        lax.ppermute(outs[step], "ctx", chip_route(step)) for step in range(1, CHIPS)
    ]
    kept = []
    handed = None
    for x_off in (1, 0):

        def sent(block, step):
            return lax.ppermute(block, "tp", ring_route(step))

        if x_off == 1:
            attended, *far = project_first(place, back, out_weight, x_off, 2)
        else:
            far = project(place, [(x_off, 2)], out_weight, attended)
        near = project(place, [(x_off, 1), (x_off, 3), (x_off, 0)], out_weight, attended)
        from_below = sent(far[0], 1)
        from_above = sent(far[1], -1)
        below_1 = sent(near[1], 1)
        above_0 = sent(near[2], -1)
        up = added(near[0], from_below).astype(jnp.bfloat16)
        down = added(near[3], from_above).astype(jnp.bfloat16)
        below_0 = sent(up, 1)
        above_1 = sent(down, -1)
        first = added(near[4], below_0, above_0)
        second = added(near[5], below_1, above_1)
        if x_off == 1:
            handed = [
                lax.ppermute(part.astype(jnp.bfloat16), "tp", PAIR_ROUTE)
                for part in (first, second)
            ]
        else:
            kept = [first, second]
    attention_out = jnp.concatenate(
        [(kept[i] + handed[i].astype(jnp.float32)).astype(jnp.bfloat16) for i in range(2)], axis=0
    )
    return (hyena_out, attention_out)


def solution(mesh):
    in_specs = (
        P("ctx", "tp"),
        P("ctx", "tp"),
        P("ctx", "tp"),
        P("tp", None),
        P("tp"),
        P("ctx", "tp"),
        P("ctx", "tp"),
        P("ctx", "tp"),
        P(None, "tp"),
    )
    out_specs = (P("ctx", "tp"), P("tp", "ctx"))
    return jax.shard_map(local_step, mesh=mesh, in_specs=in_specs, out_specs=out_specs, check_vma=False)
```

```python
import jax
import jax.numpy as jnp
from jax import lax
from jax.experimental import pallas as pl
from jax.experimental.pallas import tpu as pltpu
from jax.sharding import PartitionSpec as P

HEAD_DIM = 128
CHIPS_Y = 4
CHIPS = 8
RING = 4
NEGATIVE = -1e30
EXP_SCALE = HEAD_DIM ** (-0.5) * 1.4426950408889634


VMEM = pltpu.VMEM
SMEM_SPEC = pl.BlockSpec(memory_space=pltpu.SMEM)
VMEM_SPEC = pl.BlockSpec(memory_space=pltpu.VMEM)


def shifted(block, axis, distance):
    devices = range(lax.axis_size(axis))
    route = [(i - distance, i) for i in devices if i - distance in devices]
    return lax.ppermute(block, axis, route)


LANES = 128


def gated_blocks(query, taps, gain, out, product, first_row):
    length = taps.shape[1] // 2
    groups = taps.shape[0]
    tables = []
    for group in range(groups):
        row = jnp.broadcast_to(taps[group : group + 1, :], (length, 2 * length))
        tables.append(pltpu.roll(row, 0, 1, stride=1, stride_axis=0).astype(jnp.bfloat16))
    table = jnp.concatenate(tables, axis=0)
    lane_group = lax.broadcasted_iota(jnp.int32, (length, LANES), 1) // (LANES // groups)
    for first in range(0, product.shape[0] - length, length):
        spread = jnp.dot(
            table, product[first : first + 2 * length, :], preferred_element_type=jnp.float32
        )
        convolved = spread[:length]
        for group in range(1, groups):
            convolved = jnp.where(
                lane_group == group, spread[group * length : (group + 1) * length], convolved
            )
        here = slice(first_row + first, first_row + first + length)
        current = product[first + length : first + 2 * length, :].astype(jnp.float32)
        out[here, :] = (
            query[here, :].astype(jnp.float32) * (convolved + gain[...] * current)
        ).astype(jnp.bfloat16)


def rounded_product(left, right):
    return (left.astype(jnp.float32) * right.astype(jnp.float32)).astype(jnp.bfloat16)


def inner_kernel(query, key, value, taps, gain, out, product):
    length = taps.shape[1] // 2
    product[...] = rounded_product(key[...], value[...])
    out[:length, :] = query[:length, :]
    gated_blocks(query, taps, gain, out, product, length)


def edge_kernel(query, key, value, before, taps, gain, unused, out, product):
    length = before.shape[0]
    product[:length, :] = before[...]
    product[length:, :] = rounded_product(key[...], value[...])
    gated_blocks(query, taps, gain, out, product, 0)


def spread_taps(conv_filter):
    groups, length = conv_filter.shape
    return jnp.concatenate(
        [
            jnp.zeros((groups, 1), jnp.float32),
            conv_filter[:, ::-1].astype(jnp.float32),
            jnp.zeros((groups, length - 1), jnp.float32),
        ],
        axis=1,
    )


def columns(height):
    return pl.BlockSpec((height, LANES), lambda i: (0, i))


def hyena_inner(hyena_query, hyena_key, hyena_value, taps, gain):
    rows, width = hyena_query.shape
    steps = width // LANES
    tap_spec = pl.BlockSpec((taps.shape[0] // steps, taps.shape[1]), lambda i: (i, 0))
    return pl.pallas_call(
        inner_kernel,
        grid=(steps,),
        out_shape=jax.ShapeDtypeStruct((rows, width), jnp.bfloat16),
        in_specs=[columns(rows)] * 3 + [tap_spec, columns(1)],
        out_specs=columns(rows),
        scratch_shapes=[VMEM((rows, LANES), jnp.bfloat16)],
        cost_estimate=pl.CostEstimate(
            flops=3_000_000_000, bytes_accessed=3_000_000, transcendentals=0
        ),
        name="hyena_inner",
    )(hyena_query, hyena_key, hyena_value, taps, gain)


def hyena_edge(hyena_query, hyena_key, hyena_value, before, taps, gain, inner):
    rows, width = hyena_query.shape
    length = before.shape[0]
    steps = width // LANES
    tap_spec = pl.BlockSpec((taps.shape[0] // steps, taps.shape[1]), lambda i: (i, 0))
    return pl.pallas_call(
        edge_kernel,
        grid=(steps,),
        out_shape=jax.ShapeDtypeStruct((rows, width), jnp.bfloat16),
        in_specs=[columns(length)] * 4
        + [tap_spec, columns(1), pl.BlockSpec(memory_space=pl.ANY)],
        out_specs=columns(length),
        scratch_shapes=[VMEM((2 * length, LANES), jnp.bfloat16)],
        input_output_aliases={6: 0},
        cost_estimate=pl.CostEstimate(
            flops=1_500_000_000, bytes_accessed=1_000_000, transcendentals=0
        ),
        name="hyena_edge",
    )(hyena_query, hyena_key, hyena_value, before, taps, gain, inner)


def chip_route(step):
    route = []
    for source in range(2 * CHIPS):
        y, x, core = source // 4, source // 2 % 2, source % 2
        target = ((y + step // 2) % CHIPS_Y * 2 + (x + step) % 2) * 2 + core
        route.append((source, target))
    return route


CORE_GROUPS = [list(range(core, 2 * CHIPS, 2)) for core in range(2)]
CORE_ROUTE = [(i, i ^ 1) for i in range(2 * CHIPS)]


def ring_route(step):
    return [(i, i // RING * RING + (i + step) % RING) for i in range(2 * RING)]


PAIR_ROUTE = [(i, (i + RING) % (2 * RING)) for i in range(2 * RING)]


def ahead(y, x, step):
    return ((y + step // 2) & 3) * 2 + ((x + step) & 1)


def behind(y, x, step):
    return ((y - step // 2) & 3) * 2 + ((x - step) & 1)


def split_kernel(*refs):
    out_ref = refs[-1]
    rows = refs[0].shape[0]
    for head in range(out_ref.shape[0]):
        columns = slice(head * HEAD_DIM, (head + 1) * HEAD_DIM)
        for i, ref in enumerate(refs[:-1]):
            out_ref[head, i * rows : (i + 1) * rows, :] = ref[:, columns]


def split_heads(*arrays):
    rows = arrays[0].shape[0]
    at_once = 4
    spec = pl.BlockSpec((rows, at_once * HEAD_DIM), lambda step: (0, step))
    tall = len(arrays) * rows
    return pl.pallas_call(
        split_kernel,
        grid=(CHIPS // at_once,),
        out_shape=jax.ShapeDtypeStruct((CHIPS, tall, HEAD_DIM), jnp.bfloat16),
        in_specs=[spec] * len(arrays),
        out_specs=pl.BlockSpec((at_once, tall, HEAD_DIM), lambda step: (step, 0, 0)),
        name="split_heads",
    )(*arrays)


def attention_kernel(place, own, other, *refs):
    outs = refs[:CHIPS]
    keys, values, top, total, even, odd = refs[CHIPS:]
    y, x, core = place[0], place[1], place[2]
    step = pl.program_id(0)
    rows = top.shape[0]

    @pl.when(step == 0)
    def _():
        ones = jnp.ones((2 * rows, HEAD_DIM), jnp.bfloat16)
        for i in range(CHIPS):
            keys[i, :, :rows] = own[i, :rows, :].T
            keys[i, :, rows:] = other[i, :rows, :].T
            values[i, :rows, :HEAD_DIM] = own[i, rows : 2 * rows, :]
            values[i, rows:, :HEAD_DIM] = other[i, rows:, :]
            values[i, :, HEAD_DIM:] = ones

    top[...] = jnp.full_like(top, NEGATIVE)
    total[...] = jnp.zeros_like(total)
    chip = ahead(y, x, step)

    def score(held, block):
        held[...] = jnp.dot(
            own[chip, 2 * rows :, :], keys[block], preferred_element_type=jnp.float32
        )

    def weigh(held, block, masked):
        scores = held[...]
        if masked:
            row = lax.broadcasted_iota(jnp.int32, scores.shape, 0)
            column = lax.broadcasted_iota(jnp.int32, scores.shape, 1)
            limit = rows + core * rows
            allowed = (column <= row) | ((column >= rows) & (column < limit))
            scores = jnp.where(allowed, scores, NEGATIVE)
        old = top[...]
        new = jnp.maximum(old, jnp.max(scores, axis=1, keepdims=True))
        keep = jnp.exp2((old - new) * EXP_SCALE)
        spread = jnp.concatenate([new] * (2 * rows // HEAD_DIM), axis=1)
        weights = jnp.exp2((scores - spread) * EXP_SCALE).astype(jnp.bfloat16)
        total[...] = total[...] * jnp.concatenate([keep, keep], axis=1) + jnp.dot(
            weights, values[block], preferred_element_type=jnp.float32
        )
        top[...] = new

    score(even, 0)

    def two_blocks(pair, unused):
        score(odd, 2 * pair + 1)
        weigh(even, 2 * pair, False)
        score(even, 2 * pair + 2)
        weigh(odd, 2 * pair + 1, False)
        return unused

    lax.fori_loop(0, chip >> 1, two_blocks, 0)

    @pl.when((chip & 1) == 0)
    def _():
        weigh(even, chip, True)

    @pl.when((chip & 1) == 1)
    def _():
        score(odd, chip)
        weigh(even, chip - 1, False)
        weigh(odd, chip, True)

    result = (total[:, :HEAD_DIM] / total[:, HEAD_DIM:]).astype(jnp.bfloat16)
    for i in range(CHIPS):

        @pl.when(step == i)
        def _(i=i):
            outs[i][...] = result


def attention(place, own, other):
    rows = own.shape[1] // 3
    return pl.pallas_call(
        attention_kernel,
        grid=(CHIPS,),
        out_shape=[jax.ShapeDtypeStruct((rows, HEAD_DIM), jnp.bfloat16)] * CHIPS,
        in_specs=[SMEM_SPEC, VMEM_SPEC, VMEM_SPEC],
        out_specs=[VMEM_SPEC] * CHIPS,
        scratch_shapes=[
            VMEM((CHIPS, HEAD_DIM, 2 * rows), jnp.bfloat16),
            VMEM((CHIPS, 2 * rows, 2 * HEAD_DIM), jnp.bfloat16),
            VMEM((rows, HEAD_DIM), jnp.float32),
            VMEM((rows, 2 * HEAD_DIM), jnp.float32),
            VMEM((rows, 2 * rows), jnp.float32),
            VMEM((rows, 2 * rows), jnp.float32),
        ],
        cost_estimate=pl.CostEstimate(
            flops=12_000_000_000, bytes_accessed=6_000_000, transcendentals=10_000_000
        ),
        name="attention",
    )(place, own, other)


def project_first(place, pieces, out_weight, x_off, z_off):
    rows = pieces[0].shape[0]
    share = out_weight.shape[0] // (2 * RING)
    features = out_weight.shape[1]

    def weight_block(step, place):
        return (((place[3] + x_off) & 1) * RING + ((place[4] + z_off) & 3), 0)

    def kernel(place, weight_ref, *refs):
        joined, block = refs[CHIPS:]
        for step in range(CHIPS):
            column = pl.multiple_of(behind(place[0], place[1], step) * HEAD_DIM, HEAD_DIM)
            joined[:, pl.ds(column, HEAD_DIM)] = refs[step][...]
        piece = lax.dot_general(
            joined[...],
            weight_ref[...],
            (((1,), (1,)), ((), ())),
            preferred_element_type=jnp.float32,
        )
        block[...] = piece.astype(jnp.bfloat16).T

    def whole(height, width):
        return pl.BlockSpec((height, width), lambda step, place: (0, 0))

    return pl.pallas_call(
        kernel,
        grid_spec=pltpu.PrefetchScalarGridSpec(
            num_scalar_prefetch=1,
            grid=(1,),
            in_specs=[pl.BlockSpec((share, features), weight_block)]
            + [whole(rows, HEAD_DIM)] * CHIPS,
            out_specs=[whole(rows, features), whole(share, rows)],
        ),
        out_shape=[
            jax.ShapeDtypeStruct((rows, features), jnp.bfloat16),
            jax.ShapeDtypeStruct((share, rows), jnp.bfloat16),
        ],
        cost_estimate=pl.CostEstimate(
            flops=2 * share * rows * features,
            bytes_accessed=share * features * 2,
            transcendentals=0,
        ),
        name="project_first",
    )(place, out_weight, *pieces)


def project(place, wanted, out_weight, attended):
    rows, features = attended.shape
    share = out_weight.shape[0] // (2 * RING)
    count = len(wanted)
    heights = [share // parts for _, _, parts in wanted for _ in range(parts)]

    def weight_block(step, place):
        index = jnp.int32(0)
        for i, (x_off, z_off, _) in enumerate(wanted):
            block = ((place[3] + x_off) & 1) * RING + ((place[4] + z_off) & 3)
            index = jnp.where(step == i, block, index)
        return (index, 0)

    def kernel(place, weight_ref, attended_ref, *outs):
        piece = lax.dot_general(
            attended_ref[...],
            weight_ref[...],
            (((1,), (1,)), ((), ())),
            preferred_element_type=jnp.float32,
        )
        piece = piece.astype(jnp.bfloat16).T
        at = 0
        for i, (_, _, parts) in enumerate(wanted):
            mine = outs[at : at + parts]
            at += parts

            @pl.when(pl.program_id(0) == i)
            def _(mine=mine):
                height = share // len(mine)
                for part, out in enumerate(mine):
                    out[...] = piece[part * height : (part + 1) * height]

    return pl.pallas_call(
        kernel,
        grid_spec=pltpu.PrefetchScalarGridSpec(
            num_scalar_prefetch=1,
            grid=(count,),
            in_specs=[
                pl.BlockSpec((share, features), weight_block),
                pl.BlockSpec((rows, features), lambda step, place: (0, 0)),
            ],
            out_specs=[
                pl.BlockSpec((height, rows), lambda step, place: (0, 0)) for height in heights
            ],
        ),
        out_shape=[jax.ShapeDtypeStruct((height, rows), jnp.bfloat16) for height in heights],
        cost_estimate=pl.CostEstimate(
            flops=2 * share * rows * features * count,
            bytes_accessed=share * features * 2 * count,
            transcendentals=0,
        ),
        name="project",
    )(place, out_weight, attended)


def added(*pieces):
    return sum(piece.astype(jnp.float32) for piece in pieces)


def local_step(
    hyena_query,
    hyena_key,
    hyena_value,
    conv_filter,
    skip_gain,
    query_rows,
    key_rows,
    value_rows,
    out_weight,
):
    ctx = lax.axis_index("ctx")
    tp = lax.axis_index("tp")
    place = jnp.stack([ctx // 4, ctx // 2 % 2, ctx % 2, tp // RING, tp % RING])
    place = place.astype(jnp.int32)

    rows = query_rows.shape[0]
    length = conv_filter.shape[1]
    tail = (
        hyena_key[rows - length :].astype(jnp.float32)
        * hyena_value[rows - length :].astype(jnp.float32)
    ).astype(jnp.bfloat16)
    pieces = split_heads(key_rows, value_rows, query_rows)
    own = lax.all_to_all(pieces, "ctx", 0, 0, axis_index_groups=CORE_GROUPS, tiled=True)
    before = shifted(tail, "ctx", 1)
    taps = spread_taps(conv_filter)
    gain = skip_gain[None, :]
    inner = hyena_inner(hyena_query, hyena_key, hyena_value, taps, gain)
    hyena_out = hyena_edge(hyena_query, hyena_key, hyena_value, before, taps, gain, inner)
    other = lax.ppermute(own[:, : 2 * rows], "ctx", CORE_ROUTE)
    outs = attention(place, own, other)
    back = [outs[0]] + [
        lax.ppermute(outs[step], "ctx", chip_route(step)) for step in range(1, CHIPS)
    ]

    def sent(block, step):
        return lax.ppermute(block, "tp", ring_route(step))

    attended, far = project_first(place, back, out_weight, 1, 2)
    crossed = lax.ppermute(far, "tp", PAIR_ROUTE)
    up, down = project(place, [(1, 1, 1), (1, 3, 1)], out_weight, attended)
    from_below = sent(up, 1)
    from_above = sent(down, -1)
    far_0, far_1, up_0, up_1, down_0, down_1, other_own = project(
        place, [(0, 2, 2), (0, 1, 2), (0, 3, 2), (1, 0, 1)], out_weight, attended
    )
    half = far_0.shape[0]
    first_below = sent(added(far_0, crossed[:half]).astype(jnp.bfloat16), 1)
    first_above = sent(added(far_1, crossed[half:]).astype(jnp.bfloat16), -1)
    below_1 = sent(up_1, 1)
    above_0 = sent(down_0, -1)
    handed = lax.ppermute(
        added(other_own, from_below, from_above).astype(jnp.bfloat16), "tp", PAIR_ROUTE
    )
    own_0, own_1 = project(place, [(0, 0, 2)], out_weight, attended)
    below_0 = sent(added(up_0, first_below).astype(jnp.bfloat16), 1)
    above_1 = sent(added(down_1, first_above).astype(jnp.bfloat16), -1)
    attention_out = jnp.concatenate(
        [
            added(own_0, below_0, above_0, handed[:half]).astype(jnp.bfloat16),
            added(own_1, below_1, above_1, handed[half:]).astype(jnp.bfloat16),
        ],
        axis=0,
    )
    return (hyena_out, attention_out)


def solution(mesh):
    in_specs = (
        P("ctx", "tp"),
        P("ctx", "tp"),
        P("ctx", "tp"),
        P("tp", None),
        P("tp"),
        P("ctx", "tp"),
        P("ctx", "tp"),
        P("ctx", "tp"),
        P(None, "tp"),
    )
    out_specs = (P("ctx", "tp"), P("tp", "ctx"))
    return jax.shard_map(local_step, mesh=mesh, in_specs=in_specs, out_specs=out_specs, check_vma=False)
```

```python
import jax
import jax.numpy as jnp
from jax import lax
from jax.experimental import pallas as pl
from jax.experimental.pallas import tpu as pltpu
from jax.sharding import PartitionSpec as P

HEAD_DIM = 128
CHIPS_Y = 4
CHIPS = 8
RING = 4
NEGATIVE = -1e30
EXP_SCALE = HEAD_DIM ** (-0.5) * 1.4426950408889634


VMEM = pltpu.VMEM
SMEM_SPEC = pl.BlockSpec(memory_space=pltpu.SMEM)
VMEM_SPEC = pl.BlockSpec(memory_space=pltpu.VMEM)


def shifted(block, axis, distance):
    devices = range(lax.axis_size(axis))
    route = [(i - distance, i) for i in devices if i - distance in devices]
    return lax.ppermute(block, axis, route)


LANES = 128


def gated_blocks(query, taps, gain, out, product, first_row):
    length = taps.shape[1] // 2
    groups = taps.shape[0]
    tables = []
    for group in range(groups):
        row = jnp.broadcast_to(taps[group : group + 1, :], (length, 2 * length))
        tables.append(pltpu.roll(row, 0, 1, stride=1, stride_axis=0).astype(jnp.bfloat16))
    table = jnp.concatenate(tables, axis=0)
    lane_group = lax.broadcasted_iota(jnp.int32, (length, LANES), 1) // (LANES // groups)
    for first in range(0, product.shape[0] - length, length):
        spread = jnp.dot(
            table, product[first : first + 2 * length, :], preferred_element_type=jnp.float32
        )
        convolved = spread[:length]
        for group in range(1, groups):
            convolved = jnp.where(
                lane_group == group, spread[group * length : (group + 1) * length], convolved
            )
        here = slice(first_row + first, first_row + first + length)
        current = product[first + length : first + 2 * length, :].astype(jnp.float32)
        out[here, :] = (
            query[here, :].astype(jnp.float32) * (convolved + gain[...] * current)
        ).astype(jnp.bfloat16)


def rounded_product(left, right):
    return (left.astype(jnp.float32) * right.astype(jnp.float32)).astype(jnp.bfloat16)


def inner_kernel(query, key, value, taps, gain, out, product):
    length = taps.shape[1] // 2
    product[...] = rounded_product(key[...], value[...])
    out[:length, :] = query[:length, :]
    gated_blocks(query, taps, gain, out, product, length)


def edge_kernel(query, key, value, before, taps, gain, unused, out, product):
    length = before.shape[0]
    product[:length, :] = before[...]
    product[length:, :] = rounded_product(key[...], value[...])
    gated_blocks(query, taps, gain, out, product, 0)


def spread_taps(conv_filter):
    groups, length = conv_filter.shape
    return jnp.concatenate(
        [
            jnp.zeros((groups, 1), jnp.float32),
            conv_filter[:, ::-1].astype(jnp.float32),
            jnp.zeros((groups, length - 1), jnp.float32),
        ],
        axis=1,
    )


def columns(height):
    return pl.BlockSpec((height, LANES), lambda i: (0, i))


def hyena_inner(hyena_query, hyena_key, hyena_value, taps, gain):
    rows, width = hyena_query.shape
    steps = width // LANES
    tap_spec = pl.BlockSpec((taps.shape[0] // steps, taps.shape[1]), lambda i: (i, 0))
    return pl.pallas_call(
        inner_kernel,
        grid=(steps,),
        out_shape=jax.ShapeDtypeStruct((rows, width), jnp.bfloat16),
        in_specs=[columns(rows)] * 3 + [tap_spec, columns(1)],
        out_specs=columns(rows),
        scratch_shapes=[VMEM((rows, LANES), jnp.bfloat16)],
        cost_estimate=pl.CostEstimate(
            flops=3_000_000_000, bytes_accessed=3_000_000, transcendentals=0
        ),
        name="hyena_inner",
    )(hyena_query, hyena_key, hyena_value, taps, gain)


def hyena_edge(hyena_query, hyena_key, hyena_value, before, taps, gain, inner):
    rows, width = hyena_query.shape
    length = before.shape[0]
    steps = width // LANES
    tap_spec = pl.BlockSpec((taps.shape[0] // steps, taps.shape[1]), lambda i: (i, 0))
    return pl.pallas_call(
        edge_kernel,
        grid=(steps,),
        out_shape=jax.ShapeDtypeStruct((rows, width), jnp.bfloat16),
        in_specs=[columns(length)] * 4
        + [tap_spec, columns(1), pl.BlockSpec(memory_space=pl.ANY)],
        out_specs=columns(length),
        scratch_shapes=[VMEM((2 * length, LANES), jnp.bfloat16)],
        input_output_aliases={6: 0},
        cost_estimate=pl.CostEstimate(
            flops=1_500_000_000, bytes_accessed=1_000_000, transcendentals=0
        ),
        name="hyena_edge",
    )(hyena_query, hyena_key, hyena_value, before, taps, gain, inner)


def chip_route(step):
    route = []
    for source in range(2 * CHIPS):
        y, x, core = source // 4, source // 2 % 2, source % 2
        target = ((y + step // 2) % CHIPS_Y * 2 + (x + step) % 2) * 2 + core
        route.append((source, target))
    return route


CORE_GROUPS = [list(range(core, 2 * CHIPS, 2)) for core in range(2)]
CORE_ROUTE = [(i, i ^ 1) for i in range(2 * CHIPS)]


def ring_route(step):
    return [(i, i // RING * RING + (i + step) % RING) for i in range(2 * RING)]


PAIR_ROUTE = [(i, (i + RING) % (2 * RING)) for i in range(2 * RING)]


def ahead(y, x, step):
    return ((y + step // 2) & 3) * 2 + ((x + step) & 1)


def behind(y, x, step):
    return ((y - step // 2) & 3) * 2 + ((x - step) & 1)


def split_kernel(*refs):
    out_ref = refs[-1]
    rows = refs[0].shape[0]
    for head in range(out_ref.shape[0]):
        columns = slice(head * HEAD_DIM, (head + 1) * HEAD_DIM)
        for i, ref in enumerate(refs[:-1]):
            out_ref[head, i * rows : (i + 1) * rows, :] = ref[:, columns]


def split_heads(*arrays):
    rows = arrays[0].shape[0]
    at_once = 4
    spec = pl.BlockSpec((rows, at_once * HEAD_DIM), lambda step: (0, step))
    tall = len(arrays) * rows
    return pl.pallas_call(
        split_kernel,
        grid=(CHIPS // at_once,),
        out_shape=jax.ShapeDtypeStruct((CHIPS, tall, HEAD_DIM), jnp.bfloat16),
        in_specs=[spec] * len(arrays),
        out_specs=pl.BlockSpec((at_once, tall, HEAD_DIM), lambda step: (step, 0, 0)),
        name="split_heads",
    )(*arrays)


def attention_kernel(place, own, other, *refs):
    outs = refs[:CHIPS]
    keys, values, top, total, even, odd = refs[CHIPS:]
    y, x, core = place[0], place[1], place[2]
    step = pl.program_id(0)
    rows = top.shape[0]

    @pl.when(step == 0)
    def _():
        ones = jnp.ones((2 * rows, HEAD_DIM), jnp.bfloat16)
        for i in range(CHIPS):
            keys[i, :, :rows] = own[i, :rows, :].T
            keys[i, :, rows:] = other[i, :rows, :].T
            values[i, :rows, :HEAD_DIM] = own[i, rows : 2 * rows, :]
            values[i, rows:, :HEAD_DIM] = other[i, rows:, :]
            values[i, :, HEAD_DIM:] = ones

    top[...] = jnp.full_like(top, NEGATIVE)
    total[...] = jnp.zeros_like(total)
    chip = ahead(y, x, step)

    def score(held, block):
        held[...] = jnp.dot(
            own[chip, 2 * rows :, :], keys[block], preferred_element_type=jnp.float32
        )

    def weigh(held, block, masked):
        scores = held[...]
        if masked:
            row = lax.broadcasted_iota(jnp.int32, scores.shape, 0)
            column = lax.broadcasted_iota(jnp.int32, scores.shape, 1)
            limit = rows + core * rows
            allowed = (column <= row) | ((column >= rows) & (column < limit))
            scores = jnp.where(allowed, scores, NEGATIVE)
        old = top[...]
        new = jnp.maximum(old, jnp.max(scores, axis=1, keepdims=True))
        keep = jnp.exp2((old - new) * EXP_SCALE)
        spread = jnp.concatenate([new] * (2 * rows // HEAD_DIM), axis=1)
        weights = jnp.exp2((scores - spread) * EXP_SCALE).astype(jnp.bfloat16)
        total[...] = total[...] * jnp.concatenate([keep, keep], axis=1) + jnp.dot(
            weights, values[block], preferred_element_type=jnp.float32
        )
        top[...] = new

    score(even, 0)

    def two_blocks(pair, unused):
        score(odd, 2 * pair + 1)
        weigh(even, 2 * pair, False)
        score(even, 2 * pair + 2)
        weigh(odd, 2 * pair + 1, False)
        return unused

    lax.fori_loop(0, chip >> 1, two_blocks, 0)

    @pl.when((chip & 1) == 0)
    def _():
        weigh(even, chip, True)

    @pl.when((chip & 1) == 1)
    def _():
        score(odd, chip)
        weigh(even, chip - 1, False)
        weigh(odd, chip, True)

    result = (total[:, :HEAD_DIM] / total[:, HEAD_DIM:]).astype(jnp.bfloat16)
    for i in range(CHIPS):

        @pl.when(step == i)
        def _(i=i):
            outs[i][...] = result


def attention(place, own, other):
    rows = own.shape[1] // 3
    return pl.pallas_call(
        attention_kernel,
        grid=(CHIPS,),
        out_shape=[jax.ShapeDtypeStruct((rows, HEAD_DIM), jnp.bfloat16)] * CHIPS,
        in_specs=[SMEM_SPEC, VMEM_SPEC, VMEM_SPEC],
        out_specs=[VMEM_SPEC] * CHIPS,
        scratch_shapes=[
            VMEM((CHIPS, HEAD_DIM, 2 * rows), jnp.bfloat16),
            VMEM((CHIPS, 2 * rows, 2 * HEAD_DIM), jnp.bfloat16),
            VMEM((rows, HEAD_DIM), jnp.float32),
            VMEM((rows, 2 * HEAD_DIM), jnp.float32),
            VMEM((rows, 2 * rows), jnp.float32),
            VMEM((rows, 2 * rows), jnp.float32),
        ],
        cost_estimate=pl.CostEstimate(
            flops=12_000_000_000, bytes_accessed=6_000_000, transcendentals=10_000_000
        ),
        name="attention",
    )(place, own, other)


def project(place, wanted, out_weight, attended=None, pieces=()):
    rows = (pieces[0] if pieces else attended).shape[0]
    features = out_weight.shape[1]
    share = out_weight.shape[0] // (2 * RING)
    count = len(wanted)
    heights = [share // parts for _, _, parts in wanted for _ in range(parts)]

    def weight_block(step, place):
        index = jnp.int32(0)
        for i, (x_off, z_off, _) in enumerate(wanted):
            block = ((place[3] + x_off) & 1) * RING + ((place[4] + z_off) & 3)
            index = jnp.where(step == i, block, index)
        return (index, 0)

    def kernel(place, weight_ref, *refs):
        if pieces:
            joined, *outs = refs[CHIPS:]

            @pl.when(pl.program_id(0) == 0)
            def _():
                for step in range(CHIPS):
                    column = behind(place[0], place[1], step) * HEAD_DIM
                    column = pl.multiple_of(column, HEAD_DIM)
                    joined[:, pl.ds(column, HEAD_DIM)] = refs[step][...]

        else:
            joined, *outs = refs
        piece = lax.dot_general(
            joined[...],
            weight_ref[...],
            (((1,), (1,)), ((), ())),
            preferred_element_type=jnp.float32,
        )
        piece = piece.astype(jnp.bfloat16).T
        at = 0
        for i, (_, _, parts) in enumerate(wanted):
            mine = outs[at : at + parts]
            at += parts

            @pl.when(pl.program_id(0) == i)
            def _(mine=mine):
                height = share // len(mine)
                for part, out in enumerate(mine):
                    out[...] = piece[part * height : (part + 1) * height]

    def whole(height, width):
        return pl.BlockSpec((height, width), lambda step, place: (0, 0))

    outs = [((rows, features) if pieces else None)] + [(height, rows) for height in heights]
    outs = [shape for shape in outs if shape]
    inputs = [whole(rows, HEAD_DIM)] * CHIPS if pieces else [whole(rows, features)]
    return pl.pallas_call(
        kernel,
        grid_spec=pltpu.PrefetchScalarGridSpec(
            num_scalar_prefetch=1,
            grid=(count,),
            in_specs=[pl.BlockSpec((share, features), weight_block)] + inputs,
            out_specs=[whole(*shape) for shape in outs],
        ),
        out_shape=[jax.ShapeDtypeStruct(shape, jnp.bfloat16) for shape in outs],
        cost_estimate=pl.CostEstimate(
            flops=2 * share * rows * features * count,
            bytes_accessed=share * features * 2 * count,
            transcendentals=0,
        ),
        name="project",
    )(place, out_weight, *(pieces if pieces else (attended,)))


def added(*pieces):
    return sum(piece.astype(jnp.float32) for piece in pieces)


def local_step(
    hyena_query,
    hyena_key,
    hyena_value,
    conv_filter,
    skip_gain,
    query_rows,
    key_rows,
    value_rows,
    out_weight,
):
    ctx = lax.axis_index("ctx")
    tp = lax.axis_index("tp")
    place = jnp.stack([ctx // 4, ctx // 2 % 2, ctx % 2, tp // RING, tp % RING])
    place = place.astype(jnp.int32)

    rows = query_rows.shape[0]
    length = conv_filter.shape[1]
    tail = (
        hyena_key[rows - length :].astype(jnp.float32)
        * hyena_value[rows - length :].astype(jnp.float32)
    ).astype(jnp.bfloat16)
    pieces = split_heads(key_rows, value_rows, query_rows)
    own = lax.all_to_all(pieces, "ctx", 0, 0, axis_index_groups=CORE_GROUPS, tiled=True)
    before = shifted(tail, "ctx", 1)
    taps = spread_taps(conv_filter)
    gain = skip_gain[None, :]
    inner = hyena_inner(hyena_query, hyena_key, hyena_value, taps, gain)
    hyena_out = hyena_edge(hyena_query, hyena_key, hyena_value, before, taps, gain, inner)
    other = lax.ppermute(own[:, : 2 * rows], "ctx", CORE_ROUTE)
    outs = attention(place, own, other)
    back = [outs[0]] + [
        lax.ppermute(outs[step], "ctx", chip_route(step)) for step in range(1, CHIPS)
    ]

    def sent(block, step):
        return lax.ppermute(block, "tp", ring_route(step))

    attended, far, up, down = project(
        place, [(1, 2, 1), (1, 1, 1), (1, 3, 1)], out_weight, pieces=back
    )
    crossed = lax.ppermute(far, "tp", PAIR_ROUTE)
    from_below = sent(up, 1)
    from_above = sent(down, -1)
    far_0, far_1, up_0, up_1, down_0, down_1, other_own = project(
        place, [(0, 2, 2), (0, 1, 2), (0, 3, 2), (1, 0, 1)], out_weight, attended
    )
    half = far_0.shape[0]
    first_below = sent(added(far_0, crossed[:half]).astype(jnp.bfloat16), 1)
    first_above = sent(added(far_1, crossed[half:]).astype(jnp.bfloat16), -1)
    below_1 = sent(up_1, 1)
    above_0 = sent(down_0, -1)
    handed = lax.ppermute(
        added(other_own, from_below, from_above).astype(jnp.bfloat16), "tp", PAIR_ROUTE
    )
    (kept,) = project(place, [(0, 0, 1)], out_weight, attended)
    below_0 = sent(added(up_0, first_below).astype(jnp.bfloat16), 1)
    above_1 = sent(added(down_1, first_above).astype(jnp.bfloat16), -1)
    partial_out = lax.optimization_barrier(
        added(kept, jnp.concatenate([above_0, below_1], axis=0), handed)
    )
    attention_out = (
        partial_out + jnp.concatenate([below_0, above_1], axis=0).astype(jnp.float32)
    ).astype(jnp.bfloat16)
    return (hyena_out, attention_out)


def solution(mesh):
    in_specs = (
        P("ctx", "tp"),
        P("ctx", "tp"),
        P("ctx", "tp"),
        P("tp", None),
        P("tp"),
        P("ctx", "tp"),
        P("ctx", "tp"),
        P("ctx", "tp"),
        P(None, "tp"),
    )
    out_specs = (P("ctx", "tp"), P("tp", "ctx"))
    return jax.shard_map(local_step, mesh=mesh, in_specs=in_specs, out_specs=out_specs, check_vma=False)
```

```python
import jax
import jax.numpy as jnp
from jax import lax
from jax.experimental import pallas as pl
from jax.experimental.pallas import tpu as pltpu
from jax.sharding import PartitionSpec as P

HEAD_DIM = 128
CHIPS_Y = 4
CHIPS = 8
RING = 4
NEGATIVE = -1e30
EXP_SCALE = HEAD_DIM ** (-0.5) * 1.4426950408889634


VMEM = pltpu.VMEM
SMEM_SPEC = pl.BlockSpec(memory_space=pltpu.SMEM)
VMEM_SPEC = pl.BlockSpec(memory_space=pltpu.VMEM)


def shifted(block, axis, distance):
    devices = range(lax.axis_size(axis))
    route = [(i - distance, i) for i in devices if i - distance in devices]
    return lax.ppermute(block, axis, route)


LANES = 128


def gated_blocks(query, taps, gain, out, product, first_row):
    length = taps.shape[1] // 2
    groups = taps.shape[0]
    tables = []
    for group in range(groups):
        row = jnp.broadcast_to(taps[group : group + 1, :], (length, 2 * length))
        tables.append(pltpu.roll(row, 0, 1, stride=1, stride_axis=0).astype(jnp.bfloat16))
    table = jnp.concatenate(tables, axis=0)
    lane_group = lax.broadcasted_iota(jnp.int32, (length, LANES), 1) // (LANES // groups)
    for first in range(0, product.shape[0] - length, length):
        spread = jnp.dot(
            table, product[first : first + 2 * length, :], preferred_element_type=jnp.float32
        )
        convolved = spread[:length]
        for group in range(1, groups):
            convolved = jnp.where(
                lane_group == group, spread[group * length : (group + 1) * length], convolved
            )
        here = slice(first_row + first, first_row + first + length)
        current = product[first + length : first + 2 * length, :].astype(jnp.float32)
        out[here, :] = (
            query[here, :].astype(jnp.float32) * (convolved + gain[...] * current)
        ).astype(jnp.bfloat16)


def rounded_product(left, right):
    return (left.astype(jnp.float32) * right.astype(jnp.float32)).astype(jnp.bfloat16)


def inner_kernel(query, key, value, taps, gain, out, product):
    length = taps.shape[1] // 2
    product[...] = rounded_product(key[...], value[...])
    out[:length, :] = query[:length, :]
    gated_blocks(query, taps, gain, out, product, length)


def edge_kernel(query, key, value, before, taps, gain, unused, out, product):
    length = before.shape[0]
    product[:length, :] = before[...]
    product[length:, :] = rounded_product(key[...], value[...])
    gated_blocks(query, taps, gain, out, product, 0)


def spread_taps(conv_filter):
    groups, length = conv_filter.shape
    return jnp.concatenate(
        [
            jnp.zeros((groups, 1), jnp.float32),
            conv_filter[:, ::-1].astype(jnp.float32),
            jnp.zeros((groups, length - 1), jnp.float32),
        ],
        axis=1,
    )


def columns(height):
    return pl.BlockSpec((height, LANES), lambda i: (0, i))


def hyena_inner(hyena_query, hyena_key, hyena_value, taps, gain):
    rows, width = hyena_query.shape
    steps = width // LANES
    tap_spec = pl.BlockSpec((taps.shape[0] // steps, taps.shape[1]), lambda i: (i, 0))
    return pl.pallas_call(
        inner_kernel,
        grid=(steps,),
        out_shape=jax.ShapeDtypeStruct((rows, width), jnp.bfloat16),
        in_specs=[columns(rows)] * 3 + [tap_spec, columns(1)],
        out_specs=columns(rows),
        scratch_shapes=[VMEM((rows, LANES), jnp.bfloat16)],
        cost_estimate=pl.CostEstimate(
            flops=3_000_000_000, bytes_accessed=3_000_000, transcendentals=0
        ),
        name="hyena_inner",
    )(hyena_query, hyena_key, hyena_value, taps, gain)


def hyena_edge(hyena_query, hyena_key, hyena_value, before, taps, gain, inner):
    rows, width = hyena_query.shape
    length = before.shape[0]
    steps = width // LANES
    tap_spec = pl.BlockSpec((taps.shape[0] // steps, taps.shape[1]), lambda i: (i, 0))
    return pl.pallas_call(
        edge_kernel,
        grid=(steps,),
        out_shape=jax.ShapeDtypeStruct((rows, width), jnp.bfloat16),
        in_specs=[columns(length)] * 4
        + [tap_spec, columns(1), pl.BlockSpec(memory_space=pl.ANY)],
        out_specs=columns(length),
        scratch_shapes=[VMEM((2 * length, LANES), jnp.bfloat16)],
        input_output_aliases={6: 0},
        cost_estimate=pl.CostEstimate(
            flops=1_500_000_000, bytes_accessed=1_000_000, transcendentals=0
        ),
        name="hyena_edge",
    )(hyena_query, hyena_key, hyena_value, before, taps, gain, inner)


def chip_route(step):
    route = []
    for source in range(2 * CHIPS):
        y, x, core = source // 4, source // 2 % 2, source % 2
        target = ((y + step // 2) % CHIPS_Y * 2 + (x + step) % 2) * 2 + core
        route.append((source, target))
    return route


CORE_GROUPS = [list(range(core, 2 * CHIPS, 2)) for core in range(2)]
CORE_ROUTE = [(i, i ^ 1) for i in range(2 * CHIPS)]


def ring_route(step):
    return [(i, i // RING * RING + (i + step) % RING) for i in range(2 * RING)]


PAIR_ROUTE = [(i, (i + RING) % (2 * RING)) for i in range(2 * RING)]


def ahead(y, x, step):
    return ((y + step // 2) & 3) * 2 + ((x + step) & 1)


def behind(y, x, step):
    return ((y - step // 2) & 3) * 2 + ((x - step) & 1)


def split_kernel(*refs):
    out_ref = refs[-1]
    rows = refs[0].shape[0]
    for head in range(out_ref.shape[0]):
        columns = slice(head * HEAD_DIM, (head + 1) * HEAD_DIM)
        for i, ref in enumerate(refs[:-1]):
            out_ref[head, i * rows : (i + 1) * rows, :] = ref[:, columns]


def split_heads(*arrays):
    rows = arrays[0].shape[0]
    at_once = 4
    spec = pl.BlockSpec((rows, at_once * HEAD_DIM), lambda step: (0, step))
    tall = len(arrays) * rows
    return pl.pallas_call(
        split_kernel,
        grid=(CHIPS // at_once,),
        out_shape=jax.ShapeDtypeStruct((CHIPS, tall, HEAD_DIM), jnp.bfloat16),
        in_specs=[spec] * len(arrays),
        out_specs=pl.BlockSpec((at_once, tall, HEAD_DIM), lambda step: (step, 0, 0)),
        name="split_heads",
    )(*arrays)


def attention_kernel(place, own, other, *refs):
    outs = refs[:CHIPS]
    keys, values, top, total, even, odd = refs[CHIPS:]
    y, x, core = place[0], place[1], place[2]
    step = pl.program_id(0)
    rows = top.shape[0]

    @pl.when(step == 0)
    def _():
        ones = jnp.ones((2 * rows, HEAD_DIM), jnp.bfloat16)
        for i in range(CHIPS):
            keys[i, :, :rows] = own[i, :rows, :].T
            keys[i, :, rows:] = other[i, :rows, :].T
            values[i, :rows, :HEAD_DIM] = own[i, rows : 2 * rows, :]
            values[i, rows:, :HEAD_DIM] = other[i, rows:, :]
            values[i, :, HEAD_DIM:] = ones

    top[...] = jnp.full_like(top, NEGATIVE)
    total[...] = jnp.zeros_like(total)
    chip = ahead(y, x, step)

    def score(held, block):
        held[...] = jnp.dot(
            own[chip, 2 * rows :, :], keys[block], preferred_element_type=jnp.float32
        )

    def weigh(held, block, masked):
        scores = held[...]
        if masked:
            row = lax.broadcasted_iota(jnp.int32, scores.shape, 0)
            column = lax.broadcasted_iota(jnp.int32, scores.shape, 1)
            limit = rows + core * rows
            allowed = (column <= row) | ((column >= rows) & (column < limit))
            scores = jnp.where(allowed, scores, NEGATIVE)
        old = top[...]
        new = jnp.maximum(old, jnp.max(scores, axis=1, keepdims=True))
        keep = jnp.exp2((old - new) * EXP_SCALE)
        spread = jnp.concatenate([new] * (2 * rows // HEAD_DIM), axis=1)
        weights = jnp.exp2((scores - spread) * EXP_SCALE).astype(jnp.bfloat16)
        total[...] = total[...] * jnp.concatenate([keep, keep], axis=1) + jnp.dot(
            weights, values[block], preferred_element_type=jnp.float32
        )
        top[...] = new

    score(even, 0)

    def two_blocks(pair, unused):
        score(odd, 2 * pair + 1)
        weigh(even, 2 * pair, False)
        score(even, 2 * pair + 2)
        weigh(odd, 2 * pair + 1, False)
        return unused

    lax.fori_loop(0, chip >> 1, two_blocks, 0)

    @pl.when((chip & 1) == 0)
    def _():
        weigh(even, chip, True)

    @pl.when((chip & 1) == 1)
    def _():
        score(odd, chip)
        weigh(even, chip - 1, False)
        weigh(odd, chip, True)

    result = (total[:, :HEAD_DIM] / total[:, HEAD_DIM:]).astype(jnp.bfloat16)
    for i in range(CHIPS):

        @pl.when(step == i)
        def _(i=i):
            outs[i][...] = result


def attention(place, own, other):
    rows = own.shape[1] // 3
    return pl.pallas_call(
        attention_kernel,
        grid=(CHIPS,),
        out_shape=[jax.ShapeDtypeStruct((rows, HEAD_DIM), jnp.bfloat16)] * CHIPS,
        in_specs=[SMEM_SPEC, VMEM_SPEC, VMEM_SPEC],
        out_specs=[VMEM_SPEC] * CHIPS,
        scratch_shapes=[
            VMEM((CHIPS, HEAD_DIM, 2 * rows), jnp.bfloat16),
            VMEM((CHIPS, 2 * rows, 2 * HEAD_DIM), jnp.bfloat16),
            VMEM((rows, HEAD_DIM), jnp.float32),
            VMEM((rows, 2 * HEAD_DIM), jnp.float32),
            VMEM((rows, 2 * rows), jnp.float32),
            VMEM((rows, 2 * rows), jnp.float32),
        ],
        cost_estimate=pl.CostEstimate(
            flops=12_000_000_000, bytes_accessed=6_000_000, transcendentals=10_000_000
        ),
        name="attention",
    )(place, own, other)


WHOLE, HALVES = (4,), (2, 2)


def project(place, wanted, out_weight, attended=None, pieces=()):
    rows = (pieces[0] if pieces else attended).shape[0]
    features = out_weight.shape[1]
    share = out_weight.shape[0] // (2 * RING)
    count = len(wanted)
    heights = [share // 4 * part for _, _, quarters in wanted for part in quarters]

    def weight_block(step, place):
        index = jnp.int32(0)
        for i, (x_off, z_off, _) in enumerate(wanted):
            block = ((place[3] + x_off) & 1) * RING + ((place[4] + z_off) & 3)
            index = jnp.where(step == i, block, index)
        return (index, 0)

    def kernel(place, weight_ref, *refs):
        if pieces:
            joined, *outs = refs[CHIPS:]

            @pl.when(pl.program_id(0) == 0)
            def _():
                for step in range(CHIPS):
                    column = behind(place[0], place[1], step) * HEAD_DIM
                    column = pl.multiple_of(column, HEAD_DIM)
                    joined[:, pl.ds(column, HEAD_DIM)] = refs[step][...]

        else:
            joined, *outs = refs
        piece = lax.dot_general(
            joined[...],
            weight_ref[...],
            (((1,), (1,)), ((), ())),
            preferred_element_type=jnp.float32,
        )
        piece = piece.astype(jnp.bfloat16).T
        at = 0
        for i, (_, _, quarters) in enumerate(wanted):
            mine = outs[at : at + len(quarters)]
            at += len(quarters)

            @pl.when(pl.program_id(0) == i)
            def _(mine=mine):
                first = 0
                for out in mine:
                    out[...] = piece[first : first + out.shape[0]]
                    first += out.shape[0]

    def whole(height, width):
        return pl.BlockSpec((height, width), lambda step, place: (0, 0))

    outs = [((rows, features) if pieces else None)] + [(height, rows) for height in heights]
    outs = [shape for shape in outs if shape]
    inputs = [whole(rows, HEAD_DIM)] * CHIPS if pieces else [whole(rows, features)]
    return pl.pallas_call(
        kernel,
        grid_spec=pltpu.PrefetchScalarGridSpec(
            num_scalar_prefetch=1,
            grid=(count,),
            in_specs=[pl.BlockSpec((share, features), weight_block)] + inputs,
            out_specs=[whole(*shape) for shape in outs],
        ),
        out_shape=[jax.ShapeDtypeStruct(shape, jnp.bfloat16) for shape in outs],
        cost_estimate=pl.CostEstimate(
            flops=2 * share * rows * features * count,
            bytes_accessed=share * features * 2 * count,
            transcendentals=0,
        ),
        name="project",
    )(place, out_weight, *(pieces if pieces else (attended,)))


def added(*pieces):
    return sum(piece.astype(jnp.float32) for piece in pieces)


def local_step(
    hyena_query,
    hyena_key,
    hyena_value,
    conv_filter,
    skip_gain,
    query_rows,
    key_rows,
    value_rows,
    out_weight,
):
    ctx = lax.axis_index("ctx")
    tp = lax.axis_index("tp")
    place = jnp.stack([ctx // 4, ctx // 2 % 2, ctx % 2, tp // RING, tp % RING])
    place = place.astype(jnp.int32)

    rows = query_rows.shape[0]
    length = conv_filter.shape[1]
    tail = (
        hyena_key[rows - length :].astype(jnp.float32)
        * hyena_value[rows - length :].astype(jnp.float32)
    ).astype(jnp.bfloat16)
    pieces = split_heads(key_rows, value_rows, query_rows)
    own = lax.all_to_all(pieces, "ctx", 0, 0, axis_index_groups=CORE_GROUPS, tiled=True)
    before = shifted(tail, "ctx", 1)
    taps = spread_taps(conv_filter)
    gain = skip_gain[None, :]
    inner = hyena_inner(hyena_query, hyena_key, hyena_value, taps, gain)
    hyena_out = hyena_edge(hyena_query, hyena_key, hyena_value, before, taps, gain, inner)
    other = lax.ppermute(own[:, : 2 * rows], "ctx", CORE_ROUTE)
    outs = attention(place, own, other)
    back = [outs[0]] + [
        lax.ppermute(outs[step], "ctx", chip_route(step)) for step in range(1, CHIPS)
    ]

    def sent(block, step):
        return lax.ppermute(block, "tp", ring_route(step))

    attended, far, up, down = project(
        place, [(1, 2, WHOLE), (1, 1, WHOLE), (1, 3, WHOLE)], out_weight, pieces=back
    )
    crossed = lax.ppermute(far, "tp", PAIR_ROUTE)
    from_below = sent(up, 1)
    from_above = sent(down, -1)
    far_0, far_1, up_0, up_1, up_2, down_0, down_1, down_2, other_own = project(
        place,
        [(0, 2, HALVES), (0, 1, (2, 1, 1)), (0, 3, (1, 1, 2)), (1, 0, WHOLE)],
        out_weight,
        attended,
    )
    half = far_0.shape[0]
    below_1 = sent(up_1, 1)
    above_0 = sent(down_0, -1)
    first_below = sent(added(far_0, crossed[:half]).astype(jnp.bfloat16), 1)
    first_above = sent(added(far_1, crossed[half:]).astype(jnp.bfloat16), -1)
    below_2 = sent(up_2, 1)
    above_1 = sent(down_1, -1)
    handed = lax.ppermute(
        added(other_own, from_below, from_above).astype(jnp.bfloat16), "tp", PAIR_ROUTE
    )
    (kept,) = project(place, [(0, 0, WHOLE)], out_weight, attended)
    below_0 = sent(added(up_0, first_below).astype(jnp.bfloat16), 1)
    above_2 = sent(added(down_2, first_above).astype(jnp.bfloat16), -1)
    partial_out = lax.optimization_barrier(
        added(kept, jnp.concatenate([above_0, above_1, below_1, below_2], axis=0), handed)
    )
    attention_out = (
        partial_out + jnp.concatenate([below_0, above_2], axis=0).astype(jnp.float32)
    ).astype(jnp.bfloat16)
    return (hyena_out, attention_out)


def solution(mesh):
    in_specs = (
        P("ctx", "tp"),
        P("ctx", "tp"),
        P("ctx", "tp"),
        P("tp", None),
        P("tp"),
        P("ctx", "tp"),
        P("ctx", "tp"),
        P("ctx", "tp"),
        P(None, "tp"),
    )
    out_specs = (P("ctx", "tp"), P("tp", "ctx"))
    return jax.shard_map(local_step, mesh=mesh, in_specs=in_specs, out_specs=out_specs, check_vma=False)
```

```python
import jax
import jax.numpy as jnp
from jax import lax
from jax.experimental import pallas as pl
from jax.experimental.pallas import tpu as pltpu
from jax.sharding import PartitionSpec as P

HEAD_DIM = 128
CHIPS_Y = 4
CHIPS = 8
RING = 4
NEGATIVE = -1e30
EXP_SCALE = HEAD_DIM ** (-0.5) * 1.4426950408889634


VMEM = pltpu.VMEM
SMEM_SPEC = pl.BlockSpec(memory_space=pltpu.SMEM)
VMEM_SPEC = pl.BlockSpec(memory_space=pltpu.VMEM)


def shifted(block, axis, distance):
    devices = range(lax.axis_size(axis))
    route = [(i - distance, i) for i in devices if i - distance in devices]
    return lax.ppermute(block, axis, route)


LANES = 128


def gated_blocks(query, taps, gain, out, product, first_row):
    length = taps.shape[1] // 2
    groups = taps.shape[0]
    tables = []
    for group in range(groups):
        row = jnp.broadcast_to(taps[group : group + 1, :], (length, 2 * length))
        tables.append(pltpu.roll(row, 0, 1, stride=1, stride_axis=0).astype(jnp.bfloat16))
    table = jnp.concatenate(tables, axis=0)
    lane_group = lax.broadcasted_iota(jnp.int32, (length, LANES), 1) // (LANES // groups)
    for first in range(0, product.shape[0] - length, length):
        spread = jnp.dot(
            table, product[first : first + 2 * length, :], preferred_element_type=jnp.float32
        )
        convolved = spread[:length]
        for group in range(1, groups):
            convolved = jnp.where(
                lane_group == group, spread[group * length : (group + 1) * length], convolved
            )
        here = slice(first_row + first, first_row + first + length)
        current = product[first + length : first + 2 * length, :].astype(jnp.float32)
        out[here, :] = (
            query[here, :].astype(jnp.float32) * (convolved + gain[...] * current)
        ).astype(jnp.bfloat16)


def rounded_product(left, right):
    return (left.astype(jnp.float32) * right.astype(jnp.float32)).astype(jnp.bfloat16)


def inner_kernel(query, key, value, taps, gain, out, product):
    length = taps.shape[1] // 2
    product[...] = rounded_product(key[...], value[...])
    out[:length, :] = query[:length, :]
    gated_blocks(query, taps, gain, out, product, length)


def edge_kernel(query, key, value, before, taps, gain, unused, out, product):
    length = before.shape[0]
    product[:length, :] = before[...]
    product[length:, :] = rounded_product(key[...], value[...])
    gated_blocks(query, taps, gain, out, product, 0)


def spread_taps(conv_filter):
    groups, length = conv_filter.shape
    return jnp.concatenate(
        [
            jnp.zeros((groups, 1), jnp.float32),
            conv_filter[:, ::-1].astype(jnp.float32),
            jnp.zeros((groups, length - 1), jnp.float32),
        ],
        axis=1,
    )


def columns(height):
    return pl.BlockSpec((height, LANES), lambda i: (0, i))


def hyena_inner(hyena_query, hyena_key, hyena_value, taps, gain):
    rows, width = hyena_query.shape
    steps = width // LANES
    tap_spec = pl.BlockSpec((taps.shape[0] // steps, taps.shape[1]), lambda i: (i, 0))
    return pl.pallas_call(
        inner_kernel,
        grid=(steps,),
        out_shape=jax.ShapeDtypeStruct((rows, width), jnp.bfloat16),
        in_specs=[columns(rows)] * 3 + [tap_spec, columns(1)],
        out_specs=columns(rows),
        scratch_shapes=[VMEM((rows, LANES), jnp.bfloat16)],
        cost_estimate=pl.CostEstimate(
            flops=3_000_000_000, bytes_accessed=3_000_000, transcendentals=0
        ),
        name="hyena_inner",
    )(hyena_query, hyena_key, hyena_value, taps, gain)


def hyena_edge(hyena_query, hyena_key, hyena_value, before, taps, gain, inner):
    rows, width = hyena_query.shape
    length = before.shape[0]
    steps = width // LANES
    tap_spec = pl.BlockSpec((taps.shape[0] // steps, taps.shape[1]), lambda i: (i, 0))
    return pl.pallas_call(
        edge_kernel,
        grid=(steps,),
        out_shape=jax.ShapeDtypeStruct((rows, width), jnp.bfloat16),
        in_specs=[columns(length)] * 4
        + [tap_spec, columns(1), pl.BlockSpec(memory_space=pl.ANY)],
        out_specs=columns(length),
        scratch_shapes=[VMEM((2 * length, LANES), jnp.bfloat16)],
        input_output_aliases={6: 0},
        cost_estimate=pl.CostEstimate(
            flops=1_500_000_000, bytes_accessed=1_000_000, transcendentals=0
        ),
        name="hyena_edge",
    )(hyena_query, hyena_key, hyena_value, before, taps, gain, inner)


def chip_route(step):
    route = []
    for source in range(2 * CHIPS):
        y, x, core = source // 4, source // 2 % 2, source % 2
        target = ((y + step // 2) % CHIPS_Y * 2 + (x + step) % 2) * 2 + core
        route.append((source, target))
    return route


CORE_ROUTE = [(i, i ^ 1) for i in range(2 * CHIPS)]


def ring_route(step):
    return [(i, i // RING * RING + (i + step) % RING) for i in range(2 * RING)]


PAIR_ROUTE = [(i, (i + RING) % (2 * RING)) for i in range(2 * RING)]


def ahead(y, x, step):
    return ((y + step // 2) & 3) * 2 + ((x + step) & 1)


def behind(y, x, step):
    return ((y - step // 2) & 3) * 2 + ((x - step) & 1)


def split_kernel(k_ref, v_ref, q_ref, *outs):
    ctx = lax.axis_index("ctx")
    y, x = ctx // 4, ctx // 2 % 2
    rows = k_ref.shape[0]
    for step in range(CHIPS):
        column = pl.multiple_of(ahead(y, x, step) * HEAD_DIM, HEAD_DIM)
        for i, ref in enumerate((k_ref, v_ref, q_ref)):
            outs[step][i * rows : (i + 1) * rows, :] = ref[:, pl.ds(column, HEAD_DIM)]


def split_heads(key_rows, value_rows, query_rows):
    rows = key_rows.shape[0]
    return pl.pallas_call(
        split_kernel,
        out_shape=[jax.ShapeDtypeStruct((3 * rows, HEAD_DIM), jnp.bfloat16)] * CHIPS,
        in_specs=[VMEM_SPEC] * 3,
        out_specs=[VMEM_SPEC] * CHIPS,
        name="split_heads",
    )(key_rows, value_rows, query_rows)


def attention_kernel(place, *refs):
    own = refs[:CHIPS]
    other = refs[CHIPS : 2 * CHIPS]
    outs = refs[2 * CHIPS : 3 * CHIPS]
    queries, keys, values, top, total, even, odd = refs[3 * CHIPS :]
    y, x, core = place[0], place[1], place[2]
    step = pl.program_id(0)
    rows = top.shape[0]

    @pl.when(step == 0)
    def _():
        ones = jnp.ones((2 * rows, HEAD_DIM), jnp.bfloat16)
        for i in range(CHIPS):
            chip = behind(y, x, i)
            queries[chip] = own[i][2 * rows :, :]
            keys[chip, :, :rows] = own[i][:rows, :].T
            keys[chip, :, rows:] = other[i][:rows, :].T
            values[chip, :rows, :HEAD_DIM] = own[i][rows : 2 * rows, :]
            values[chip, rows:, :HEAD_DIM] = other[i][rows : 2 * rows, :]
            values[chip, :, HEAD_DIM:] = ones

    top[...] = jnp.full_like(top, NEGATIVE)
    total[...] = jnp.zeros_like(total)
    chip = ahead(y, x, step)

    def score(held, block):
        held[...] = jnp.dot(
            queries[chip], keys[block], preferred_element_type=jnp.float32
        )

    def weigh(held, block, masked):
        scores = held[...]
        if masked:
            row = lax.broadcasted_iota(jnp.int32, scores.shape, 0)
            column = lax.broadcasted_iota(jnp.int32, scores.shape, 1)
            limit = rows + core * rows
            allowed = (column <= row) | ((column >= rows) & (column < limit))
            scores = jnp.where(allowed, scores, NEGATIVE)
        old = top[...]
        new = jnp.maximum(old, jnp.max(scores, axis=1, keepdims=True))
        keep = jnp.exp2((old - new) * EXP_SCALE)
        spread = jnp.concatenate([new] * (2 * rows // HEAD_DIM), axis=1)
        weights = jnp.exp2((scores - spread) * EXP_SCALE).astype(jnp.bfloat16)
        total[...] = total[...] * jnp.concatenate([keep, keep], axis=1) + jnp.dot(
            weights, values[block], preferred_element_type=jnp.float32
        )
        top[...] = new

    score(even, 0)

    def two_blocks(pair, unused):
        score(odd, 2 * pair + 1)
        weigh(even, 2 * pair, False)
        score(even, 2 * pair + 2)
        weigh(odd, 2 * pair + 1, False)
        return unused

    lax.fori_loop(0, chip >> 1, two_blocks, 0)

    @pl.when((chip & 1) == 0)
    def _():
        weigh(even, chip, True)

    @pl.when((chip & 1) == 1)
    def _():
        score(odd, chip)
        weigh(even, chip - 1, False)
        weigh(odd, chip, True)

    result = (total[:, :HEAD_DIM] / total[:, HEAD_DIM:]).astype(jnp.bfloat16)
    for i in range(CHIPS):

        @pl.when(step == i)
        def _(i=i):
            outs[i][...] = result


def attention(place, own, other):
    rows = own[0].shape[0] // 3
    return pl.pallas_call(
        attention_kernel,
        grid=(CHIPS,),
        out_shape=[jax.ShapeDtypeStruct((rows, HEAD_DIM), jnp.bfloat16)] * CHIPS,
        in_specs=[SMEM_SPEC] + [VMEM_SPEC] * (2 * CHIPS),
        out_specs=[VMEM_SPEC] * CHIPS,
        scratch_shapes=[
            VMEM((CHIPS, rows, HEAD_DIM), jnp.bfloat16),
            VMEM((CHIPS, HEAD_DIM, 2 * rows), jnp.bfloat16),
            VMEM((CHIPS, 2 * rows, 2 * HEAD_DIM), jnp.bfloat16),
            VMEM((rows, HEAD_DIM), jnp.float32),
            VMEM((rows, 2 * HEAD_DIM), jnp.float32),
            VMEM((rows, 2 * rows), jnp.float32),
            VMEM((rows, 2 * rows), jnp.float32),
        ],
        cost_estimate=pl.CostEstimate(
            flops=12_000_000_000, bytes_accessed=6_000_000, transcendentals=10_000_000
        ),
        name="attention",
    )(place, *own, *other)


def project(place, wanted, out_weight, attended=None, pieces=()):
    rows = (pieces[0] if pieces else attended).shape[0]
    features = out_weight.shape[1]
    share = out_weight.shape[0] // (2 * RING)
    count = len(wanted)
    heights = [share // parts for _, _, parts in wanted for _ in range(parts)]

    def weight_block(step, place):
        index = jnp.int32(0)
        for i, (x_off, z_off, _) in enumerate(wanted):
            block = ((place[3] + x_off) & 1) * RING + ((place[4] + z_off) & 3)
            index = jnp.where(step == i, block, index)
        return (index, 0)

    def kernel(place, weight_ref, *refs):
        if pieces:
            joined, *outs = refs[CHIPS:]

            @pl.when(pl.program_id(0) == 0)
            def _():
                for step in range(CHIPS):
                    column = behind(place[0], place[1], step) * HEAD_DIM
                    column = pl.multiple_of(column, HEAD_DIM)
                    joined[:, pl.ds(column, HEAD_DIM)] = refs[step][...]

        else:
            joined, *outs = refs
        piece = lax.dot_general(
            joined[...],
            weight_ref[...],
            (((1,), (1,)), ((), ())),
            preferred_element_type=jnp.float32,
        )
        piece = piece.astype(jnp.bfloat16).T
        at = 0
        for i, (_, _, parts) in enumerate(wanted):
            mine = outs[at : at + parts]
            at += parts

            @pl.when(pl.program_id(0) == i)
            def _(mine=mine):
                height = share // len(mine)
                for part, out in enumerate(mine):
                    out[...] = piece[part * height : (part + 1) * height]

    def whole(height, width):
        return pl.BlockSpec((height, width), lambda step, place: (0, 0))

    outs = [((rows, features) if pieces else None)] + [(height, rows) for height in heights]
    outs = [shape for shape in outs if shape]
    inputs = [whole(rows, HEAD_DIM)] * CHIPS if pieces else [whole(rows, features)]
    return pl.pallas_call(
        kernel,
        grid_spec=pltpu.PrefetchScalarGridSpec(
            num_scalar_prefetch=1,
            grid=(count,),
            in_specs=[pl.BlockSpec((share, features), weight_block)] + inputs,
            out_specs=[whole(*shape) for shape in outs],
        ),
        out_shape=[jax.ShapeDtypeStruct(shape, jnp.bfloat16) for shape in outs],
        cost_estimate=pl.CostEstimate(
            flops=2 * share * rows * features * count,
            bytes_accessed=share * features * 2 * count,
            transcendentals=0,
        ),
        name="project",
    )(place, out_weight, *(pieces if pieces else (attended,)))


def added(*pieces):
    return sum(piece.astype(jnp.float32) for piece in pieces)


def local_step(
    hyena_query,
    hyena_key,
    hyena_value,
    conv_filter,
    skip_gain,
    query_rows,
    key_rows,
    value_rows,
    out_weight,
):
    ctx = lax.axis_index("ctx")
    tp = lax.axis_index("tp")
    place = jnp.stack([ctx // 4, ctx // 2 % 2, ctx % 2, tp // RING, tp % RING])
    place = place.astype(jnp.int32)

    rows = query_rows.shape[0]
    length = conv_filter.shape[1]
    pieces = split_heads(key_rows, value_rows, query_rows)
    own = [pieces[0]] + [
        lax.ppermute(pieces[step], "ctx", chip_route(step)) for step in range(1, CHIPS)
    ]
    taps = spread_taps(conv_filter)
    gain = skip_gain[None, :]
    inner = hyena_inner(hyena_query, hyena_key, hyena_value, taps, gain)
    other = [lax.ppermute(block, "ctx", CORE_ROUTE) for block in own]
    outs = attention(place, own, other)
    back = [outs[0]] + [
        lax.ppermute(outs[step], "ctx", chip_route(step)) for step in range(1, CHIPS)
    ]
    tail_key, tail_value, _ = lax.optimization_barrier(
        (hyena_key[rows - length :], hyena_value[rows - length :], outs[0])
    )
    before = shifted(rounded_product(tail_key, tail_value), "ctx", 1)
    hyena_out = hyena_edge(hyena_query, hyena_key, hyena_value, before, taps, gain, inner)

    def sent(block, step):
        return lax.ppermute(block, "tp", ring_route(step))

    attended, far, up, down = project(
        place, [(1, 2, 1), (1, 1, 1), (1, 3, 1)], out_weight, pieces=back
    )
    crossed = lax.ppermute(far, "tp", PAIR_ROUTE)
    from_below = sent(up, 1)
    from_above = sent(down, -1)
    far_0, far_1, up_0, up_1, down_0, down_1, other_own = project(
        place, [(0, 2, 2), (0, 1, 2), (0, 3, 2), (1, 0, 1)], out_weight, attended
    )
    half = far_0.shape[0]
    first_below = sent(added(far_0, crossed[:half]).astype(jnp.bfloat16), 1)
    first_above = sent(added(far_1, crossed[half:]).astype(jnp.bfloat16), -1)
    below_1 = sent(up_1, 1)
    above_0 = sent(down_0, -1)
    handed = lax.ppermute(
        added(other_own, from_below, from_above).astype(jnp.bfloat16), "tp", PAIR_ROUTE
    )
    (kept,) = project(place, [(0, 0, 1)], out_weight, attended)
    below_0 = sent(added(up_0, first_below).astype(jnp.bfloat16), 1)
    above_1 = sent(added(down_1, first_above).astype(jnp.bfloat16), -1)
    partial_out = lax.optimization_barrier(
        added(kept, jnp.concatenate([above_0, below_1], axis=0), handed)
    )
    attention_out = (
        partial_out + jnp.concatenate([below_0, above_1], axis=0).astype(jnp.float32)
    ).astype(jnp.bfloat16)
    return (hyena_out, attention_out)


def solution(mesh):
    in_specs = (
        P("ctx", "tp"),
        P("ctx", "tp"),
        P("ctx", "tp"),
        P("tp", None),
        P("tp"),
        P("ctx", "tp"),
        P("ctx", "tp"),
        P("ctx", "tp"),
        P(None, "tp"),
    )
    out_specs = (P("ctx", "tp"), P("tp", "ctx"))
    return jax.shard_map(local_step, mesh=mesh, in_specs=in_specs, out_specs=out_specs, check_vma=False)
```

```python
import jax
import jax.numpy as jnp
from jax import lax
from jax.experimental import pallas as pl
from jax.experimental.pallas import tpu as pltpu
from jax.sharding import PartitionSpec as P

HEAD_DIM = 128
CHIPS_Y = 4
CHIPS = 8
RING = 4
NEGATIVE = -1e30
EXP_SCALE = HEAD_DIM ** (-0.5) * 1.4426950408889634


VMEM = pltpu.VMEM
SMEM_SPEC = pl.BlockSpec(memory_space=pltpu.SMEM)
VMEM_SPEC = pl.BlockSpec(memory_space=pltpu.VMEM)


def shifted(block, axis, distance):
    devices = range(lax.axis_size(axis))
    route = [(i - distance, i) for i in devices if i - distance in devices]
    return lax.ppermute(block, axis, route)


LANES = 128


def gated_blocks(query, taps, gain, out, product, first_row):
    length = taps.shape[1] // 2
    groups = taps.shape[0]
    tables = []
    for group in range(groups):
        row = jnp.broadcast_to(taps[group : group + 1, :], (length, 2 * length))
        tables.append(pltpu.roll(row, 0, 1, stride=1, stride_axis=0).astype(jnp.bfloat16))
    table = jnp.concatenate(tables, axis=0)
    lane_group = lax.broadcasted_iota(jnp.int32, (length, LANES), 1) // (LANES // groups)
    for first in range(0, product.shape[0] - length, length):
        spread = jnp.dot(
            table, product[first : first + 2 * length, :], preferred_element_type=jnp.float32
        )
        convolved = spread[:length]
        for group in range(1, groups):
            convolved = jnp.where(
                lane_group == group, spread[group * length : (group + 1) * length], convolved
            )
        here = slice(first_row + first, first_row + first + length)
        current = product[first + length : first + 2 * length, :].astype(jnp.float32)
        out[here, :] = (
            query[here, :].astype(jnp.float32) * (convolved + gain[...] * current)
        ).astype(jnp.bfloat16)


def rounded_product(left, right):
    return (left.astype(jnp.float32) * right.astype(jnp.float32)).astype(jnp.bfloat16)


def inner_kernel(query, key, value, taps, gain, out, product):
    length = taps.shape[1] // 2
    product[...] = rounded_product(key[...], value[...])
    out[:length, :] = query[:length, :]
    gated_blocks(query, taps, gain, out, product, length)


def edge_kernel(query, key, value, before, taps, gain, unused, out, product):
    length = before.shape[0]
    product[:length, :] = before[...]
    product[length:, :] = rounded_product(key[...], value[...])
    gated_blocks(query, taps, gain, out, product, 0)


def spread_taps(conv_filter):
    groups, length = conv_filter.shape
    return jnp.concatenate(
        [
            jnp.zeros((groups, 1), jnp.float32),
            conv_filter[:, ::-1].astype(jnp.float32),
            jnp.zeros((groups, length - 1), jnp.float32),
        ],
        axis=1,
    )


def columns(height):
    return pl.BlockSpec((height, LANES), lambda i: (0, i))


def hyena_inner(hyena_query, hyena_key, hyena_value, taps, gain):
    rows, width = hyena_query.shape
    steps = width // LANES
    tap_spec = pl.BlockSpec((taps.shape[0] // steps, taps.shape[1]), lambda i: (i, 0))
    return pl.pallas_call(
        inner_kernel,
        grid=(steps,),
        out_shape=jax.ShapeDtypeStruct((rows, width), jnp.bfloat16),
        in_specs=[columns(rows)] * 3 + [tap_spec, columns(1)],
        out_specs=columns(rows),
        scratch_shapes=[VMEM((rows, LANES), jnp.bfloat16)],
        cost_estimate=pl.CostEstimate(
            flops=3_000_000_000, bytes_accessed=3_000_000, transcendentals=0
        ),
        name="hyena_inner",
    )(hyena_query, hyena_key, hyena_value, taps, gain)


def hyena_edge(hyena_query, hyena_key, hyena_value, before, taps, gain, inner):
    rows, width = hyena_query.shape
    length = before.shape[0]
    steps = width // LANES
    tap_spec = pl.BlockSpec((taps.shape[0] // steps, taps.shape[1]), lambda i: (i, 0))
    return pl.pallas_call(
        edge_kernel,
        grid=(steps,),
        out_shape=jax.ShapeDtypeStruct((rows, width), jnp.bfloat16),
        in_specs=[columns(length)] * 4
        + [tap_spec, columns(1), pl.BlockSpec(memory_space=pl.ANY)],
        out_specs=columns(length),
        scratch_shapes=[VMEM((2 * length, LANES), jnp.bfloat16)],
        input_output_aliases={6: 0},
        cost_estimate=pl.CostEstimate(
            flops=1_500_000_000, bytes_accessed=1_000_000, transcendentals=0
        ),
        name="hyena_edge",
    )(hyena_query, hyena_key, hyena_value, before, taps, gain, inner)


def chip_route(step):
    route = []
    for source in range(2 * CHIPS):
        y, x, core = source // 4, source // 2 % 2, source % 2
        target = ((y + step // 2) % CHIPS_Y * 2 + (x + step) % 2) * 2 + core
        route.append((source, target))
    return route


CORE_ROUTE = [(i, i ^ 1) for i in range(2 * CHIPS)]


def ring_route(step):
    return [(i, i // RING * RING + (i + step) % RING) for i in range(2 * RING)]


PAIR_ROUTE = [(i, (i + RING) % (2 * RING)) for i in range(2 * RING)]


def ahead(y, x, step):
    return ((y + step // 2) & 3) * 2 + ((x + step) & 1)


def behind(y, x, step):
    return ((y - step // 2) & 3) * 2 + ((x - step) & 1)


def split_kernel(k_ref, v_ref, q_ref, *outs):
    ctx = lax.axis_index("ctx")
    y, x = ctx // 4, ctx // 2 % 2
    rows = k_ref.shape[0]
    for step in range(CHIPS):
        column = pl.multiple_of(ahead(y, x, step) * HEAD_DIM, HEAD_DIM)
        for i, ref in enumerate((k_ref, v_ref, q_ref)):
            outs[step][i * rows : (i + 1) * rows, :] = ref[:, pl.ds(column, HEAD_DIM)]


def split_heads(key_rows, value_rows, query_rows):
    rows, width = key_rows.shape
    half = pl.BlockSpec((rows // 2, width), lambda part: (part, 0))
    out = pl.BlockSpec((3 * rows // 2, HEAD_DIM), lambda part: (part, 0))
    return pl.pallas_call(
        split_kernel,
        grid=(2,),
        out_shape=[jax.ShapeDtypeStruct((3 * rows, HEAD_DIM), jnp.bfloat16)] * CHIPS,
        in_specs=[half] * 3,
        out_specs=[out] * CHIPS,
        name="split_heads",
    )(key_rows, value_rows, query_rows)


def attention_kernel(place, *refs):
    own = refs[:CHIPS]
    other = refs[CHIPS : 2 * CHIPS]
    outs = refs[2 * CHIPS : 3 * CHIPS]
    queries, keys, values, top, total, even, odd = refs[3 * CHIPS :]
    y, x, core = place[0], place[1], place[2]
    step = pl.program_id(0)
    rows = top.shape[0]
    half = rows // 2

    @pl.when(step == 0)
    def _():
        ones = jnp.ones((2 * rows, HEAD_DIM), jnp.bfloat16)
        for i in range(CHIPS):
            chip = behind(y, x, i)
            for part in range(2):
                first = part * 3 * half
                here = slice(part * half, (part + 1) * half)
                there = slice(rows + part * half, rows + (part + 1) * half)
                queries[chip, here, :] = own[i][first + 2 * half : first + 3 * half, :]
                for ref, place_of in ((own[i], here), (other[i], there)):
                    values[chip, place_of, :HEAD_DIM] = ref[first + half : first + 2 * half, :]
            for ref, first in ((own[i], 0), (other[i], rows)):
                joined = jnp.concatenate([ref[:half, :], ref[3 * half : 4 * half, :]], axis=0)
                keys[chip, :, first : first + rows] = joined.T
            values[chip, :, HEAD_DIM:] = ones

    top[...] = jnp.full_like(top, NEGATIVE)
    total[...] = jnp.zeros_like(total)
    chip = ahead(y, x, step)

    def score(held, block):
        held[...] = jnp.dot(
            queries[chip], keys[block], preferred_element_type=jnp.float32
        )

    def weigh(held, block, masked):
        scores = held[...]
        if masked:
            row = lax.broadcasted_iota(jnp.int32, scores.shape, 0)
            column = lax.broadcasted_iota(jnp.int32, scores.shape, 1)
            limit = rows + core * rows
            allowed = (column <= row) | ((column >= rows) & (column < limit))
            scores = jnp.where(allowed, scores, NEGATIVE)
        old = top[...]
        new = jnp.maximum(old, jnp.max(scores, axis=1, keepdims=True))
        keep = jnp.exp2((old - new) * EXP_SCALE)
        spread = jnp.concatenate([new] * (2 * rows // HEAD_DIM), axis=1)
        weights = jnp.exp2((scores - spread) * EXP_SCALE).astype(jnp.bfloat16)
        total[...] = total[...] * jnp.concatenate([keep, keep], axis=1) + jnp.dot(
            weights, values[block], preferred_element_type=jnp.float32
        )
        top[...] = new

    score(even, 0)

    def two_blocks(pair, unused):
        score(odd, 2 * pair + 1)
        weigh(even, 2 * pair, False)
        score(even, 2 * pair + 2)
        weigh(odd, 2 * pair + 1, False)
        return unused

    lax.fori_loop(0, chip >> 1, two_blocks, 0)

    @pl.when((chip & 1) == 0)
    def _():
        weigh(even, chip, True)

    @pl.when((chip & 1) == 1)
    def _():
        score(odd, chip)
        weigh(even, chip - 1, False)
        weigh(odd, chip, True)

    result = (total[:, :HEAD_DIM] / total[:, HEAD_DIM:]).astype(jnp.bfloat16)
    for i in range(CHIPS):

        @pl.when(step == i)
        def _(i=i):
            outs[i][...] = result


def attention(place, own, other):
    rows = own[0].shape[0] // 3
    return pl.pallas_call(
        attention_kernel,
        grid=(CHIPS,),
        out_shape=[jax.ShapeDtypeStruct((rows, HEAD_DIM), jnp.bfloat16)] * CHIPS,
        in_specs=[SMEM_SPEC] + [VMEM_SPEC] * (2 * CHIPS),
        out_specs=[VMEM_SPEC] * CHIPS,
        scratch_shapes=[
            VMEM((CHIPS, rows, HEAD_DIM), jnp.bfloat16),
            VMEM((CHIPS, HEAD_DIM, 2 * rows), jnp.bfloat16),
            VMEM((CHIPS, 2 * rows, 2 * HEAD_DIM), jnp.bfloat16),
            VMEM((rows, HEAD_DIM), jnp.float32),
            VMEM((rows, 2 * HEAD_DIM), jnp.float32),
            VMEM((rows, 2 * rows), jnp.float32),
            VMEM((rows, 2 * rows), jnp.float32),
        ],
        cost_estimate=pl.CostEstimate(
            flops=12_000_000_000, bytes_accessed=6_000_000, transcendentals=10_000_000
        ),
        name="attention",
    )(place, *own, *other)


def project(place, wanted, out_weight, attended=None, pieces=()):
    rows = (pieces[0] if pieces else attended).shape[0]
    features = out_weight.shape[1]
    share = out_weight.shape[0] // (2 * RING)
    count = len(wanted)
    heights = [share // parts for _, _, parts in wanted for _ in range(parts)]

    def weight_block(step, place):
        index = jnp.int32(0)
        for i, (x_off, z_off, _) in enumerate(wanted):
            block = ((place[3] + x_off) & 1) * RING + ((place[4] + z_off) & 3)
            index = jnp.where(step == i, block, index)
        return (index, 0)

    def kernel(place, weight_ref, *refs):
        if pieces:
            joined, *outs = refs[CHIPS:]

            @pl.when(pl.program_id(0) == 0)
            def _():
                for step in range(CHIPS):
                    column = behind(place[0], place[1], step) * HEAD_DIM
                    column = pl.multiple_of(column, HEAD_DIM)
                    joined[:, pl.ds(column, HEAD_DIM)] = refs[step][...]

        else:
            joined, *outs = refs
        piece = lax.dot_general(
            joined[...],
            weight_ref[...],
            (((1,), (1,)), ((), ())),
            preferred_element_type=jnp.float32,
        )
        piece = piece.astype(jnp.bfloat16).T
        at = 0
        for i, (_, _, parts) in enumerate(wanted):
            mine = outs[at : at + parts]
            at += parts

            @pl.when(pl.program_id(0) == i)
            def _(mine=mine):
                height = share // len(mine)
                for part, out in enumerate(mine):
                    out[...] = piece[part * height : (part + 1) * height]

    def whole(height, width):
        return pl.BlockSpec((height, width), lambda step, place: (0, 0))

    outs = [((rows, features) if pieces else None)] + [(height, rows) for height in heights]
    outs = [shape for shape in outs if shape]
    inputs = [whole(rows, HEAD_DIM)] * CHIPS if pieces else [whole(rows, features)]
    return pl.pallas_call(
        kernel,
        grid_spec=pltpu.PrefetchScalarGridSpec(
            num_scalar_prefetch=1,
            grid=(count,),
            in_specs=[pl.BlockSpec((share, features), weight_block)] + inputs,
            out_specs=[whole(*shape) for shape in outs],
        ),
        out_shape=[jax.ShapeDtypeStruct(shape, jnp.bfloat16) for shape in outs],
        cost_estimate=pl.CostEstimate(
            flops=2 * share * rows * features * count,
            bytes_accessed=share * features * 2 * count,
            transcendentals=0,
        ),
        name="project",
    )(place, out_weight, *(pieces if pieces else (attended,)))


def added(*pieces):
    return sum(piece.astype(jnp.float32) for piece in pieces)


def local_step(
    hyena_query,
    hyena_key,
    hyena_value,
    conv_filter,
    skip_gain,
    query_rows,
    key_rows,
    value_rows,
    out_weight,
):
    ctx = lax.axis_index("ctx")
    tp = lax.axis_index("tp")
    place = jnp.stack([ctx // 4, ctx // 2 % 2, ctx % 2, tp // RING, tp % RING])
    place = place.astype(jnp.int32)

    rows = query_rows.shape[0]
    length = conv_filter.shape[1]

    def brought(block, step):
        return lax.ppermute(block, "ctx", chip_route(step))

    pieces = split_heads(key_rows, value_rows, query_rows)
    own = [pieces[0]] + [brought(pieces[step], step) for step in range(1, CHIPS)]
    taps = spread_taps(conv_filter)
    gain = skip_gain[None, :]
    inner = hyena_inner(hyena_query, hyena_key, hyena_value, taps, gain)
    other = []
    for block in own:
        other.append(lax.ppermute(block, "ctx", CORE_ROUTE))
    outs = attention(place, own, other)
    back = [outs[0]] + [brought(outs[step], step) for step in range(1, CHIPS)]
    tail_key, tail_value, _ = lax.optimization_barrier(
        (hyena_key[rows - length :], hyena_value[rows - length :], outs[0])
    )
    before = shifted(rounded_product(tail_key, tail_value), "ctx", 1)
    hyena_out = hyena_edge(hyena_query, hyena_key, hyena_value, before, taps, gain, inner)

    def sent(block, step):
        return lax.ppermute(block, "tp", ring_route(step))

    attended, far, up, down = project(
        place, [(1, 2, 1), (1, 1, 1), (1, 3, 1)], out_weight, pieces=back
    )
    crossed = lax.ppermute(far, "tp", PAIR_ROUTE)
    from_below = sent(up, 1)
    from_above = sent(down, -1)
    far_0, far_1, up_0, up_1, down_0, down_1, other_own = project(
        place, [(0, 2, 2), (0, 1, 2), (0, 3, 2), (1, 0, 1)], out_weight, attended
    )
    half = far_0.shape[0]
    first_below = sent(added(far_0, crossed[:half]).astype(jnp.bfloat16), 1)
    first_above = sent(added(far_1, crossed[half:]).astype(jnp.bfloat16), -1)
    below_1 = sent(up_1, 1)
    above_0 = sent(down_0, -1)
    handed = lax.ppermute(
        added(other_own, from_below, from_above).astype(jnp.bfloat16), "tp", PAIR_ROUTE
    )
    (kept,) = project(place, [(0, 0, 1)], out_weight, attended)
    below_0 = sent(added(up_0, first_below).astype(jnp.bfloat16), 1)
    above_1 = sent(added(down_1, first_above).astype(jnp.bfloat16), -1)
    partial_out = lax.optimization_barrier(
        added(kept, jnp.concatenate([above_0, below_1], axis=0), handed)
    )
    attention_out = (
        partial_out + jnp.concatenate([below_0, above_1], axis=0).astype(jnp.float32)
    ).astype(jnp.bfloat16)
    return (hyena_out, attention_out)


def solution(mesh):
    in_specs = (
        P("ctx", "tp"),
        P("ctx", "tp"),
        P("ctx", "tp"),
        P("tp", None),
        P("tp"),
        P("ctx", "tp"),
        P("ctx", "tp"),
        P("ctx", "tp"),
        P(None, "tp"),
    )
    out_specs = (P("ctx", "tp"), P("tp", "ctx"))
    return jax.shard_map(local_step, mesh=mesh, in_specs=in_specs, out_specs=out_specs, check_vma=False)
```

```python
import jax
import jax.numpy as jnp
from jax import lax
from jax.experimental import pallas as pl
from jax.experimental.pallas import tpu as pltpu
from jax.sharding import PartitionSpec as P

HEAD_DIM = 128
CHIPS_Y = 4
CHIPS = 8
RING = 4
NEGATIVE = -1e30
EXP_SCALE = HEAD_DIM ** (-0.5) * 1.4426950408889634


VMEM = pltpu.VMEM
SMEM_SPEC = pl.BlockSpec(memory_space=pltpu.SMEM)
VMEM_SPEC = pl.BlockSpec(memory_space=pltpu.VMEM)


def shifted(block, axis, distance):
    devices = range(lax.axis_size(axis))
    route = [(i - distance, i) for i in devices if i - distance in devices]
    return lax.ppermute(block, axis, route)


LANES = 128


def gated_blocks(query, taps, gain, out, product, first_row):
    length = taps.shape[1] // 2
    groups = taps.shape[0]
    tables = []
    for group in range(groups):
        row = jnp.broadcast_to(taps[group : group + 1, :], (length, 2 * length))
        tables.append(pltpu.roll(row, 0, 1, stride=1, stride_axis=0).astype(jnp.bfloat16))
    table = jnp.concatenate(tables, axis=0)
    lane_group = lax.broadcasted_iota(jnp.int32, (length, LANES), 1) // (LANES // groups)
    for first in range(0, product.shape[0] - length, length):
        spread = jnp.dot(
            table, product[first : first + 2 * length, :], preferred_element_type=jnp.float32
        )
        convolved = spread[:length]
        for group in range(1, groups):
            convolved = jnp.where(
                lane_group == group, spread[group * length : (group + 1) * length], convolved
            )
        here = slice(first_row + first, first_row + first + length)
        current = product[first + length : first + 2 * length, :].astype(jnp.float32)
        out[here, :] = (
            query[here, :].astype(jnp.float32) * (convolved + gain[...] * current)
        ).astype(jnp.bfloat16)


def rounded_product(left, right):
    return (left.astype(jnp.float32) * right.astype(jnp.float32)).astype(jnp.bfloat16)


def inner_kernel(query, key, value, taps, gain, out, product):
    length = taps.shape[1] // 2
    product[...] = rounded_product(key[...], value[...])
    out[:length, :] = query[:length, :]
    gated_blocks(query, taps, gain, out, product, length)


def edge_kernel(query, key, value, before, taps, gain, unused, out, product):
    length = before.shape[0]
    product[:length, :] = before[...]
    product[length:, :] = rounded_product(key[...], value[...])
    gated_blocks(query, taps, gain, out, product, 0)


def spread_taps(conv_filter):
    groups, length = conv_filter.shape
    return jnp.concatenate(
        [
            jnp.zeros((groups, 1), jnp.float32),
            conv_filter[:, ::-1].astype(jnp.float32),
            jnp.zeros((groups, length - 1), jnp.float32),
        ],
        axis=1,
    )


def columns(height):
    return pl.BlockSpec((height, LANES), lambda i: (0, i))


def hyena_inner(hyena_query, hyena_key, hyena_value, taps, gain):
    rows, width = hyena_query.shape
    steps = width // LANES
    tap_spec = pl.BlockSpec((taps.shape[0] // steps, taps.shape[1]), lambda i: (i, 0))
    return pl.pallas_call(
        inner_kernel,
        grid=(steps,),
        out_shape=jax.ShapeDtypeStruct((rows, width), jnp.bfloat16),
        in_specs=[columns(rows)] * 3 + [tap_spec, columns(1)],
        out_specs=columns(rows),
        scratch_shapes=[VMEM((rows, LANES), jnp.bfloat16)],
        cost_estimate=pl.CostEstimate(
            flops=3_000_000_000, bytes_accessed=3_000_000, transcendentals=0
        ),
        name="hyena_inner",
    )(hyena_query, hyena_key, hyena_value, taps, gain)


def hyena_edge(hyena_query, hyena_key, hyena_value, before, taps, gain, inner):
    rows, width = hyena_query.shape
    length = before.shape[0]
    steps = width // LANES
    tap_spec = pl.BlockSpec((taps.shape[0] // steps, taps.shape[1]), lambda i: (i, 0))
    return pl.pallas_call(
        edge_kernel,
        grid=(steps,),
        out_shape=jax.ShapeDtypeStruct((rows, width), jnp.bfloat16),
        in_specs=[columns(length)] * 4
        + [tap_spec, columns(1), pl.BlockSpec(memory_space=pl.ANY)],
        out_specs=columns(length),
        scratch_shapes=[VMEM((2 * length, LANES), jnp.bfloat16)],
        input_output_aliases={6: 0},
        cost_estimate=pl.CostEstimate(
            flops=1_500_000_000, bytes_accessed=1_000_000, transcendentals=0
        ),
        name="hyena_edge",
    )(hyena_query, hyena_key, hyena_value, before, taps, gain, inner)


def chip_route(step):
    route = []
    for source in range(2 * CHIPS):
        y, x, core = source // 4, source // 2 % 2, source % 2
        target = ((y + step // 2) % CHIPS_Y * 2 + (x + step) % 2) * 2 + core
        route.append((source, target))
    return route


CORE_ROUTE = [(i, i ^ 1) for i in range(2 * CHIPS)]


def ring_route(step):
    return [(i, i // RING * RING + (i + step) % RING) for i in range(2 * RING)]


PAIR_ROUTE = [(i, (i + RING) % (2 * RING)) for i in range(2 * RING)]


def ahead(y, x, step):
    return ((y + step // 2) & 3) * 2 + ((x + step) & 1)


def behind(y, x, step):
    return ((y - step // 2) & 3) * 2 + ((x - step) & 1)


def split_kernel(k_ref, v_ref, q_ref, *outs):
    ctx = lax.axis_index("ctx")
    y, x = ctx // 4, ctx // 2 % 2
    rows = k_ref.shape[0]
    for step in range(CHIPS):
        column = pl.multiple_of(ahead(y, x, step) * HEAD_DIM, HEAD_DIM)
        for i, ref in enumerate((k_ref, v_ref, q_ref)):
            outs[step][i * rows : (i + 1) * rows, :] = ref[:, pl.ds(column, HEAD_DIM)]


def split_heads(key_rows, value_rows, query_rows):
    rows, width = key_rows.shape
    half = pl.BlockSpec((rows // 2, width), lambda part: (part, 0))
    out = pl.BlockSpec((3 * rows // 2, HEAD_DIM), lambda part: (part, 0))
    return pl.pallas_call(
        split_kernel,
        grid=(2,),
        out_shape=[jax.ShapeDtypeStruct((3 * rows, HEAD_DIM), jnp.bfloat16)] * CHIPS,
        in_specs=[half] * 3,
        out_specs=[out] * CHIPS,
        name="split_heads",
    )(key_rows, value_rows, query_rows)


def attention_kernel(place, *refs):
    own = refs[:CHIPS]
    other = refs[CHIPS : 2 * CHIPS]
    outs = refs[2 * CHIPS : 3 * CHIPS]
    queries, keys, values, top, total, even, odd = refs[3 * CHIPS :]
    y, x, core = place[0], place[1], place[2]
    step = pl.program_id(0)
    rows = top.shape[0]
    half = rows // 2

    @pl.when(step == 0)
    def _():
        ones = jnp.ones((2 * rows, HEAD_DIM), jnp.bfloat16)
        for i in range(CHIPS):
            chip = behind(y, x, i)
            for part in range(2):
                first = part * 3 * half
                here = slice(part * half, (part + 1) * half)
                there = slice(rows + part * half, rows + (part + 1) * half)
                queries[chip, here, :] = own[i][first + 2 * half : first + 3 * half, :]
                for ref, place_of in ((own[i], here), (other[i], there)):
                    values[chip, place_of, :HEAD_DIM] = ref[first + half : first + 2 * half, :]
            for ref, first in ((own[i], 0), (other[i], rows)):
                joined = jnp.concatenate([ref[:half, :], ref[3 * half : 4 * half, :]], axis=0)
                keys[chip, :, first : first + rows] = joined.T
            values[chip, :, HEAD_DIM:] = ones

    top[...] = jnp.full_like(top, NEGATIVE)
    total[...] = jnp.zeros_like(total)
    chip = ahead(y, x, step)

    def score(held, block):
        held[...] = jnp.dot(
            queries[chip], keys[block], preferred_element_type=jnp.float32
        )

    def weigh(held, block, masked):
        scores = held[...]
        if masked:
            row = lax.broadcasted_iota(jnp.int32, scores.shape, 0)
            column = lax.broadcasted_iota(jnp.int32, scores.shape, 1)
            limit = rows + core * rows
            allowed = (column <= row) | ((column >= rows) & (column < limit))
            scores = jnp.where(allowed, scores, NEGATIVE)
        old = top[...]
        new = jnp.maximum(old, jnp.max(scores, axis=1, keepdims=True))
        keep = jnp.exp2((old - new) * EXP_SCALE)
        spread = jnp.concatenate([new] * (2 * rows // HEAD_DIM), axis=1)
        weights = jnp.exp2((scores - spread) * EXP_SCALE).astype(jnp.bfloat16)
        total[...] = total[...] * jnp.concatenate([keep, keep], axis=1) + jnp.dot(
            weights, values[block], preferred_element_type=jnp.float32
        )
        top[...] = new

    score(even, 0)

    def two_blocks(pair, unused):
        score(odd, 2 * pair + 1)
        weigh(even, 2 * pair, False)
        score(even, 2 * pair + 2)
        weigh(odd, 2 * pair + 1, False)
        return unused

    lax.fori_loop(0, chip >> 1, two_blocks, 0)

    @pl.when((chip & 1) == 0)
    def _():
        weigh(even, chip, True)

    @pl.when((chip & 1) == 1)
    def _():
        score(odd, chip)
        weigh(even, chip - 1, False)
        weigh(odd, chip, True)

    result = (total[:, :HEAD_DIM] / total[:, HEAD_DIM:]).astype(jnp.bfloat16)
    for i in range(CHIPS):

        @pl.when(step == i)
        def _(i=i):
            outs[i][...] = result


def attention(place, own, other):
    rows = own[0].shape[0] // 3
    return pl.pallas_call(
        attention_kernel,
        grid=(CHIPS,),
        out_shape=[jax.ShapeDtypeStruct((rows, HEAD_DIM), jnp.bfloat16)] * CHIPS,
        in_specs=[SMEM_SPEC] + [VMEM_SPEC] * (2 * CHIPS),
        out_specs=[VMEM_SPEC] * CHIPS,
        scratch_shapes=[
            VMEM((CHIPS, rows, HEAD_DIM), jnp.bfloat16),
            VMEM((CHIPS, HEAD_DIM, 2 * rows), jnp.bfloat16),
            VMEM((CHIPS, 2 * rows, 2 * HEAD_DIM), jnp.bfloat16),
            VMEM((rows, HEAD_DIM), jnp.float32),
            VMEM((rows, 2 * HEAD_DIM), jnp.float32),
            VMEM((rows, 2 * rows), jnp.float32),
            VMEM((rows, 2 * rows), jnp.float32),
        ],
        cost_estimate=pl.CostEstimate(
            flops=12_000_000_000, bytes_accessed=6_000_000, transcendentals=10_000_000
        ),
        name="attention",
    )(place, *own, *other)


def project(place, wanted, out_weight, attended=None, pieces=()):
    rows = (pieces[0] if pieces else attended).shape[0]
    features = out_weight.shape[1]
    share = out_weight.shape[0] // (2 * RING)
    count = len(wanted)
    heights = [share // parts for _, _, parts in wanted for _ in range(parts)]

    def weight_block(step, place):
        index = jnp.int32(0)
        for i, (x_off, z_off, _) in enumerate(wanted):
            block = ((place[3] + x_off) & 1) * RING + ((place[4] + z_off) & 3)
            index = jnp.where(step == i, block, index)
        return (index, 0)

    def kernel(place, weight_ref, *refs):
        if pieces:
            joined, *outs = refs[CHIPS:]

            @pl.when(pl.program_id(0) == 0)
            def _():
                for step in range(CHIPS):
                    column = behind(place[0], place[1], step) * HEAD_DIM
                    column = pl.multiple_of(column, HEAD_DIM)
                    joined[:, pl.ds(column, HEAD_DIM)] = refs[step][...]

        else:
            joined, *outs = refs
        piece = lax.dot_general(
            joined[...],
            weight_ref[...],
            (((1,), (1,)), ((), ())),
            preferred_element_type=jnp.float32,
        )
        piece = piece.astype(jnp.bfloat16).T
        at = 0
        for i, (_, _, parts) in enumerate(wanted):
            mine = outs[at : at + parts]
            at += parts

            @pl.when(pl.program_id(0) == i)
            def _(mine=mine):
                height = share // len(mine)
                for part, out in enumerate(mine):
                    out[...] = piece[part * height : (part + 1) * height]

    def whole(height, width):
        return pl.BlockSpec((height, width), lambda step, place: (0, 0))

    outs = [((rows, features) if pieces else None)] + [(height, rows) for height in heights]
    outs = [shape for shape in outs if shape]
    inputs = [whole(rows, HEAD_DIM)] * CHIPS if pieces else [whole(rows, features)]
    return pl.pallas_call(
        kernel,
        grid_spec=pltpu.PrefetchScalarGridSpec(
            num_scalar_prefetch=1,
            grid=(count,),
            in_specs=[pl.BlockSpec((share, features), weight_block)] + inputs,
            out_specs=[whole(*shape) for shape in outs],
        ),
        out_shape=[jax.ShapeDtypeStruct(shape, jnp.bfloat16) for shape in outs],
        cost_estimate=pl.CostEstimate(
            flops=2 * share * rows * features * count,
            bytes_accessed=share * features * 2 * count,
            transcendentals=0,
        ),
        name="project",
    )(place, out_weight, *(pieces if pieces else (attended,)))


def added(*pieces):
    return sum(piece.astype(jnp.float32) for piece in pieces)


def local_step(
    hyena_query,
    hyena_key,
    hyena_value,
    conv_filter,
    skip_gain,
    query_rows,
    key_rows,
    value_rows,
    out_weight,
):
    ctx = lax.axis_index("ctx")
    tp = lax.axis_index("tp")
    place = jnp.stack([ctx // 4, ctx // 2 % 2, ctx % 2, tp // RING, tp % RING])
    place = place.astype(jnp.int32)

    rows = query_rows.shape[0]
    length = conv_filter.shape[1]

    def brought(block, step):
        return lax.ppermute(block, "ctx", chip_route(step))

    pieces = split_heads(key_rows, value_rows, query_rows)
    own = [pieces[0]] + [brought(pieces[step], step) for step in range(1, CHIPS)]
    taps = spread_taps(conv_filter)
    gain = skip_gain[None, :]
    inner = hyena_inner(hyena_query, hyena_key, hyena_value, taps, gain)
    other = []
    for block in own:
        other.append(lax.ppermute(block, "ctx", CORE_ROUTE))
    outs = attention(place, own, other)
    back = [outs[0]] + [brought(outs[step], step) for step in range(1, CHIPS)]
    tail_key, tail_value, _ = lax.optimization_barrier(
        (hyena_key[rows - length :], hyena_value[rows - length :], outs[0])
    )
    before = shifted(rounded_product(tail_key, tail_value), "ctx", 1)
    hyena_out = hyena_edge(hyena_query, hyena_key, hyena_value, before, taps, gain, inner)

    def sent(block, step):
        return lax.ppermute(block, "tp", ring_route(step))

    attended, far, up, down = project(
        place, [(1, 2, 1), (1, 1, 1), (1, 3, 1)], out_weight, pieces=back
    )
    crossed = lax.ppermute(far, "tp", PAIR_ROUTE)
    from_below = sent(up, 1)
    from_above = sent(down, -1)
    far_0, far_1, up_0, up_1, down_0, down_1, other_own, kept = project(
        place,
        [(0, 2, 2), (0, 1, 2), (0, 3, 2), (1, 0, 1), (0, 0, 1)],
        out_weight,
        attended,
    )
    half = far_0.shape[0]
    first_below = sent(added(far_0, crossed[:half]).astype(jnp.bfloat16), 1)
    first_above = sent(added(far_1, crossed[half:]).astype(jnp.bfloat16), -1)
    below_1 = sent(up_1, 1)
    above_0 = sent(down_0, -1)
    handed = lax.ppermute(
        added(other_own, from_below, from_above).astype(jnp.bfloat16), "tp", PAIR_ROUTE
    )
    below_0 = sent(added(up_0, first_below).astype(jnp.bfloat16), 1)
    above_1 = sent(added(down_1, first_above).astype(jnp.bfloat16), -1)
    partial_out = lax.optimization_barrier(
        added(kept, jnp.concatenate([above_0, below_1], axis=0), handed)
    )
    attention_out = (
        partial_out + jnp.concatenate([below_0, above_1], axis=0).astype(jnp.float32)
    ).astype(jnp.bfloat16)
    return (hyena_out, attention_out)


def solution(mesh):
    in_specs = (
        P("ctx", "tp"),
        P("ctx", "tp"),
        P("ctx", "tp"),
        P("tp", None),
        P("tp"),
        P("ctx", "tp"),
        P("ctx", "tp"),
        P("ctx", "tp"),
        P(None, "tp"),
    )
    out_specs = (P("ctx", "tp"), P("tp", "ctx"))
    return jax.shard_map(local_step, mesh=mesh, in_specs=in_specs, out_specs=out_specs, check_vma=False)
```
